32 devices in a mesh: dp: 8 (over y, x, core), tensor: 4 (over z).
Axes of the slice: x: 2, y: 2, z: 4, core: 2. Of those that a mesh axis runs over, the one named last changes fastest.
Arguments:
- rm_hidden: bfloat16 [8, 256, 3584], P('dp', 'tensor'), may hold values from -6 to 6
- rm_cotangent: bfloat16 [8, 256, 3584], P('dp', 'tensor'), may hold values from -6 to 6
- rm_gain: float32 [3584], replicated, may hold values from 0.25 to 1.75
- rewards: float32 [8], P('dp'), may hold values from 0.25 to 8, as said below
- visual_pos: int32 [8, 128], P('dp', 'tensor'), may hold values from 0 to 255, as said below
- bridge: bfloat16 [3584, 2048], P(None, 'tensor'), may hold values from -0.09375 to 0.09375
- img_query: bfloat16 [8, 512, 2048], P('dp', 'tensor'), may hold values from -8 to 8
- img_key: bfloat16 [8, 512, 2048], P('dp', 'tensor'), may hold values from -8 to 8
- img_value: bfloat16 [8, 512, 2048], P('dp', 'tensor'), may hold values from -6 to 6
Outputs:
- grad_query: bfloat16 [8, 512, 2048], P('dp', 'tensor')
- grad_key: bfloat16 [8, 512, 2048], P('dp', 'tensor')
- grad_value: bfloat16 [8, 512, 2048], P('dp', 'tensor')
The draws below stay inside these ranges and needn't reach their ends.
Inputs may be any that keep to these rules, and one draw needn't show every extreme that they name: `visual_pos`: strictly increasing in each sample; rows 64 * t to 64 * t + 63 of a reward sequence hold exactly 32 visual tokens, for every t. `rewards`: positive.
All inputs are finite; a program needn't handle non-finite values.
Results may differ from the reference program's by a relative error of at most 0.0082.
Values may be sent and summed in bfloat16 or wider, within the bound.
No kernel may reach another device: no remote copies, remote signals or barrier semaphores. Data moves between devices by JAX's collectives and lax.ppermute only.
A program may use at most 64 MiB of HBM per device.

```python
import jax
import jax.numpy as jnp
from jax import lax

D = 3584
HEADS = 16
HD = 128
GW = 64
SAMPLES = 8
L = 512
HW = 2048
VIS = 128
VIS_DEV = 32
RM_DEV = 64
RSEQ = 256


def draw_rewards(key, part):
    index_f = jnp.arange(SAMPLES, dtype=jnp.float32)
    ramp = 3.0 ** (index_f / max(SAMPLES - 1, 1))
    noise = jnp.exp(jax.random.uniform(key, (SAMPLES,), jnp.float32, jnp.log(0.6), jnp.log(1.6)))
    return (ramp * noise).astype(jnp.float32)


def draw_visual_pos(key, part):
    blocks = VIS // VIS_DEV
    random_ints = jax.random.randint(key, (SAMPLES, blocks, RM_DEV), 0, 2 ** 20)
    scores = random_ints * RM_DEV + jnp.arange(RM_DEV, dtype=jnp.int32)
    permuted = jnp.argsort(scores, axis=-1)
    picked = jnp.sort(permuted[:, :, :VIS_DEV], axis=-1)
    block_start = jnp.arange(blocks, dtype=jnp.int32)[None, :, None] * RM_DEV
    return (picked + block_start).reshape(SAMPLES, VIS).astype(jnp.int32)


def drawn_pair(key):
    shape = (SAMPLES, L, HEADS * HD)
    query_draw = jnp.clip(jax.random.normal(jax.random.fold_in(key, 101), shape, jnp.float32), -8.0, 8.0)
    key_draw = jnp.clip(jax.random.normal(jax.random.fold_in(key, 102), shape, jnp.float32), -8.0, 8.0)
    return (query_draw, key_draw)


def draw_img_query(key, part):
    return drawn_pair(key)[0].astype(jnp.bfloat16)


def draw_img_key(key, part):
    return drawn_pair(key)[1].astype(jnp.bfloat16)


def steps_of(own_key, extent, split, smallest, largest):
    level = 1.0
    for axis_at, shards_of in split:
        steps = jax.random.uniform(jax.random.fold_in(jax.random.fold_in(own_key, 6), axis_at), (shards_of,), jnp.float32, smallest / len(split), largest / len(split))
        level = level * jnp.repeat(jnp.exp(steps), extent[axis_at] // shards_of).reshape((-1,) + (1,) * (len(extent) - 1 - axis_at))
    return level


def bell_draw(own_key, extent, width, reach, pieces=(), kind=jnp.bfloat16):
    values = jax.random.normal(own_key, extent, jnp.float32) * width
    if len(pieces) > 0:
        values = steps_of(own_key, extent, pieces, -0.22, 0.18) * values
    return jnp.clip(values, min=-reach, max=reach).astype(kind)


def setup_inputs(seed: int = 0) -> dict:
    arg_keys = jax.random.split(jax.random.key(seed), 10)
    rm_hidden = bell_draw(arg_keys[0], (SAMPLES, RSEQ, D), 1.0, 6.0, ((0, 8), (1, 4)))
    rm_cotangent = bell_draw(arg_keys[1], (SAMPLES, RSEQ, D), 1.0, 6.0, ((0, 8), (1, 4)))
    rm_gain = jnp.clip(1.0 + 0.15 * jax.random.normal(arg_keys[2], (D,), jnp.float32), 0.25, 1.75)
    rewards = draw_rewards(jax.random.fold_in(arg_keys[9], 71), 0)
    visual_pos = draw_visual_pos(jax.random.fold_in(arg_keys[9], 71), 0)
    bridge = bell_draw(arg_keys[5], (D, HW), D ** -0.5, 0.09375, ((1, 4),))
    img_query = draw_img_query(jax.random.fold_in(arg_keys[9], 71), 0)
    img_key = draw_img_key(jax.random.fold_in(arg_keys[9], 71), 0)
    img_value = bell_draw(arg_keys[8], (SAMPLES, L, HW), 1.0, 6.0, ((0, 8), (1, 4)))
    return dict(rm_hidden=rm_hidden, rm_cotangent=rm_cotangent, rm_gain=rm_gain, rewards=rewards, visual_pos=visual_pos, bridge=bridge, img_query=img_query, img_key=img_key, img_value=img_value)


def norm_backward(hidden, cotangent, gain):
    hidden_f = hidden.astype(jnp.float32)
    scaled_cot = cotangent.astype(jnp.float32) * gain.astype(jnp.float32)
    inv_rms = lax.rsqrt(lax.optimization_barrier(jnp.mean(hidden_f * hidden_f, axis=-1, keepdims=True)) + 1e-06)
    mixed = lax.optimization_barrier(jnp.mean(hidden_f * scaled_cot, axis=-1, keepdims=True))
    return (inv_rms * scaled_cot - hidden_f * inv_rms * inv_rms * inv_rms * mixed).astype(jnp.bfloat16)

def upsample(handed):
    half_width = GW // 2
    grid_rows = handed.reshape(handed.shape[0] // half_width, half_width, handed.shape[1])
    grid_rows = jnp.repeat(jnp.repeat(grid_rows, 2, axis=0), 2, axis=1)
    return grid_rows.reshape(-1, handed.shape[1])

def attend_back(query_rows, key_rows, value_rows, grad_rows):
    seq_length = query_rows.shape[0]
    block_rows = min(512, seq_length)
    score_scale = query_rows.shape[1] ** (-0.5)

    def step(carry, block_index):
        grad_key, grad_value = carry
        first_row = (block_index * block_rows).astype(jnp.int32)
        query_block = lax.dynamic_slice_in_dim(query_rows, first_row, block_rows, 0)
        grad_block = lax.dynamic_slice_in_dim(grad_rows, first_row, block_rows, 0)
        scores = jnp.dot(query_block, key_rows.T, preferred_element_type=jnp.float32) * score_scale
        row_max = lax.optimization_barrier(jnp.max(scores, axis=1, keepdims=True))
        exp_scores = jnp.exp(scores - row_max)
        attn_weights = exp_scores / lax.optimization_barrier(jnp.sum(exp_scores, axis=1, keepdims=True))
        weights_half = attn_weights.astype(jnp.bfloat16)
        grad_weights = jnp.dot(grad_block, value_rows.T, preferred_element_type=jnp.float32)
        row_dot = lax.optimization_barrier(jnp.sum(attn_weights * grad_weights, axis=1, keepdims=True))
        grad_scores = (attn_weights * (grad_weights - row_dot)).astype(jnp.bfloat16)
        grad_query = (jnp.dot(grad_scores, key_rows, preferred_element_type=jnp.float32) * score_scale).astype(jnp.bfloat16)
        grad_key = grad_key + jnp.dot(grad_scores.T, query_block, preferred_element_type=jnp.float32)
        grad_value = grad_value + jnp.dot(weights_half.T, grad_block, preferred_element_type=jnp.float32)
        return ((grad_key, grad_value), grad_query)
    zeros_init = jnp.zeros(query_rows.shape, jnp.float32)
    carry, query_blocks = lax.scan(step, (zeros_init, zeros_init), jnp.arange(seq_length // block_rows, dtype=jnp.int32))
    grad_query = query_blocks.reshape(seq_length, -1)
    grad_key = (carry[0] * score_scale).astype(jnp.bfloat16)
    grad_value = carry[1].astype(jnp.bfloat16)
    return (grad_query, grad_key, grad_value)

def heads_backward(query_rows, key_rows, value_rows, grad_rows):
    seq_length = query_rows.shape[0]
    head_count = query_rows.shape[1] // HD

    def split_heads(array):
        return array.reshape(seq_length, head_count, HD).transpose(1, 0, 2)

    def per_head(head_items):
        return attend_back(head_items[0], head_items[1], head_items[2], head_items[3])
    head_grads = lax.map(per_head, (split_heads(query_rows), split_heads(key_rows), split_heads(value_rows), split_heads(grad_rows)))
    return tuple((grads.transpose(1, 0, 2).reshape(seq_length, head_count * HD) for grads in head_grads))

def reference(rm_hidden, rm_cotangent, rm_gain, rewards, visual_pos, bridge, img_query, img_key, img_value):
    reward_weight = rewards * SAMPLES / jnp.sum(rewards)

    def per_sample(sample_items):
        hidden, cotangent, positions, weight, query_rows, key_rows, value_rows = sample_items
        vis_hidden = jnp.take(hidden, positions.astype(jnp.int32), axis=0)
        vis_cot = jnp.take(cotangent, positions.astype(jnp.int32), axis=0)
        visual_grad = norm_backward(vis_hidden, vis_cot, rm_gain)
        handed = (jnp.dot(visual_grad, bridge, preferred_element_type=jnp.float32) * weight).astype(jnp.bfloat16)
        grad_rows = upsample(handed)
        return heads_backward(query_rows, key_rows, value_rows, grad_rows)
    outputs = lax.map(per_sample, (rm_hidden, rm_cotangent, visual_pos, reward_weight, img_query, img_key, img_value))
    return (outputs[0], outputs[1], outputs[2])
```

```python
import functools

import jax
import jax.numpy as jnp
from jax import lax
from jax.experimental import pallas as pl
from jax.experimental.pallas import tpu as pltpu
from jax.sharding import PartitionSpec as P

HD = 128
GW = 64
GROUPS = 2


def norm_backward(hidden, cotangent, gain):
    hidden_f = hidden.astype(jnp.float32)
    scaled_cot = cotangent.astype(jnp.float32) * gain
    inv_rms = lax.rsqrt(jnp.mean(hidden_f * hidden_f, axis=-1, keepdims=True) + 1e-06)
    mixed = jnp.mean(hidden_f * scaled_cot, axis=-1, keepdims=True)
    return (inv_rms * scaled_cot - hidden_f * inv_rms * inv_rms * inv_rms * mixed).astype(
        jnp.bfloat16
    )


def total_over(value, axis):
    size = lax.axis_size(axis)
    if size & (size - 1):
        return lax.psum(value, axis)
    step = 1
    while step < size:
        value = value + lax.ppermute(value, axis, [(i, i ^ step) for i in range(size)])
        step *= 2
    return value


def relayed_blocks(block, axis):
    size = lax.axis_size(axis)
    here = lax.axis_index(axis)
    upward, downward = [], []
    up = down = block
    for step in range(size - 1):
        up = lax.ppermute(up, axis, [(i, i + 1) for i in range(step, size - 1)])
        down = lax.ppermute(down, axis, [(i + 1, i) for i in range(size - 1 - step)])
        upward.append(up)
        downward.append(down)
    return [block] + [
        jnp.where(here >= k, upward[k - 1], downward[size - k - 1]) for k in range(1, size)
    ]


def attend_kernel(count, scale, chunk, *refs):
    _, handed_ref, query_ref, key_ref, value_ref = refs[:5]
    blocks = refs[5 : 4 + count]
    outs = refs[4 + count : 4 + 2 * count]
    q_s, k_s, v_s, g_s, dq_s, dk_s, dv_s = refs[4 + 2 * count :]
    rows = query_ref.shape[1]
    length = rows * count
    seen = handed_ref.shape[0] // count
    q_s[pl.ds(0, rows)] = query_ref[0]
    k_s[pl.ds(0, rows)] = key_ref[0]
    v_s[pl.ds(0, rows)] = value_ref[0]
    for j, block in enumerate(blocks, 1):
        at = pl.ds(j * rows, rows)
        q_s[at] = block[0]
        k_s[at] = block[1]
        v_s[at] = block[2]
    token = lax.broadcasted_iota(jnp.int32, (rows, seen), 0)
    source = lax.broadcasted_iota(jnp.int32, (rows, seen), 1)
    spread = jnp.where(
        (token // (2 * GW)) * (GW // 2) + (token % GW) // 2 == source, 1.0, 0.0
    ).astype(jnp.bfloat16)
    for j in range(count):
        g_s[pl.ds(j * rows, rows)] = jnp.dot(
            spread, handed_ref[pl.ds(j * seen, seen)], preferred_element_type=jnp.float32
        ).astype(jnp.bfloat16)
    dk_s[...] = jnp.zeros_like(dk_s)
    dv_s[...] = jnp.zeros_like(dv_s)
    key_rows = k_s[...]
    value_rows = v_s[...]
    key_columns = key_rows.T
    both_last = (((1,), (1,)), ((), ()))

    def step(c, carry):
        at = pl.ds(pl.multiple_of(c * chunk, chunk), chunk)
        q = q_s[at]
        g = g_s[at]
        scores = lax.dot_general(key_rows, q, both_last, preferred_element_type=jnp.float32) * scale
        exp_scores = jnp.exp(scores - jnp.max(scores, axis=0, keepdims=True))
        weights = exp_scores * (1.0 / jnp.sum(exp_scores, axis=0, keepdims=True))
        grad_weights = lax.dot_general(value_rows, g, both_last, preferred_element_type=jnp.float32)
        row_dot = jnp.sum(weights * grad_weights, axis=0, keepdims=True)
        grad_scores = (weights * (grad_weights - row_dot)).astype(jnp.bfloat16)
        dv_s[...] += jnp.dot(weights.astype(jnp.bfloat16), g, preferred_element_type=jnp.float32)
        dk_s[...] += jnp.dot(grad_scores, q, preferred_element_type=jnp.float32)
        dq = jnp.dot(key_columns, grad_scores, preferred_element_type=jnp.float32)
        dq_s[at] = (dq * scale).T.astype(jnp.bfloat16)
        return carry

    lax.fori_loop(0, length // chunk, step, 0)
    for j, out in enumerate(outs):
        at = pl.ds(j * rows, rows)
        out[0] = dq_s[at]
        out[1] = (dk_s[at] * scale).astype(jnp.bfloat16)
        out[2] = dv_s[at].astype(jnp.bfloat16)


def attend(here, handed, own, blocks, group, groups, count):
    rows = own[0].shape[1]
    local_heads = handed.shape[1] // HD
    heads = local_heads // groups
    length = rows * count
    chunk = min(256, length)
    first = group * heads
    own_spec = pl.BlockSpec((1, rows, HD), lambda h, t: (0, 0, t[0] * local_heads + first + h))
    block_spec = pl.BlockSpec((3, rows, HD), lambda h, t: (0, 0, h))
    flops = 10 * heads * length * length * HD
    return pl.pallas_call(
        functools.partial(attend_kernel, count, HD**-0.5, chunk),
        grid_spec=pltpu.PrefetchScalarGridSpec(
            num_scalar_prefetch=1,
            grid=(heads,),
            in_specs=[pl.BlockSpec((handed.shape[0], HD), lambda h, t: (0, first + h))]
            + [own_spec] * 3
            + [block_spec] * (count - 1),
            out_specs=[block_spec] * count,
            scratch_shapes=[pltpu.VMEM((length, HD), jnp.bfloat16)] * 5
            + [pltpu.VMEM((length, HD), jnp.float32)] * 2,
        ),
        out_shape=[jax.ShapeDtypeStruct((3, rows, heads * HD), jnp.bfloat16)] * count,
        cost_estimate=pl.CostEstimate(
            flops=flops,
            bytes_accessed=12 * length * heads * HD,
            transcendentals=heads * length * length,
        ),
        name=f"attend_{group}",
    )(here, handed, *own, *blocks)


def place_kernel(count, groups, *refs):
    parts = refs[1 : 1 + count * groups]
    outs = refs[1 + count * groups :]
    width = parts[0].shape[2]
    for k in range(count):

        @pl.when(pl.program_id(0) == k)
        def _():
            for g in range(groups):
                for i, out in enumerate(outs):
                    out[0, :, pl.ds(g * width, width)] = parts[k * groups + g][i]


def place(here, parts, count):
    groups = len(parts[0])
    rows, width = parts[0][0].shape[1:]
    flat = [part for ranked in parts for part in ranked]
    part_spec = pl.BlockSpec((3, rows, width), lambda k, t: (0, 0, 0))
    out_spec = pl.BlockSpec((1, rows, width * groups), lambda k, t: (0, 0, lax.rem(t[0] + k, count)))
    return pl.pallas_call(
        functools.partial(place_kernel, count, groups),
        grid_spec=pltpu.PrefetchScalarGridSpec(
            num_scalar_prefetch=1,
            grid=(count,),
            in_specs=[part_spec] * len(flat),
            out_specs=[out_spec] * 3,
        ),
        out_shape=[jax.ShapeDtypeStruct((1, rows, width * groups * count), jnp.bfloat16)] * 3,
        name="place",
    )(here, *flat)


def local(
    rm_hidden, rm_cotangent, rm_gain, rewards, visual_pos, bridge, img_query, img_key, img_value
):
    count = lax.axis_size("tensor")
    here = lax.axis_index("tensor")
    place_of = here[None].astype(jnp.int32)
    own_width = img_query.shape[2] // count
    groups = min(GROUPS, own_width // HD)
    width = own_width // groups

    def columns(array, k, g):
        first = lax.rem(here + k, count) * own_width + g * width
        return lax.dynamic_slice_in_dim(array[0], first, width, 1)

    arrived = []
    for g in range(groups):
        arrived.append(
            [
                lax.ppermute(
                    jnp.stack([columns(a, k, g) for a in (img_query, img_key, img_value)]),
                    "tensor",
                    [(i, (i + k) % count) for i in range(count)],
                )
                for k in range(1, count)
            ]
        )

    reward_sum = total_over(jnp.sum(rewards), "dp")
    sample_count = lax.axis_size("dp") * rewards.shape[0]
    reward_weight = rewards[0] * sample_count / reward_sum
    row_offset = here * rm_hidden.shape[1]
    local_rows = visual_pos[0] - row_offset
    vis_hidden = jnp.take(rm_hidden[0], local_rows, axis=0)
    vis_cot = jnp.take(rm_cotangent[0], local_rows, axis=0)
    visual_grad = norm_backward(vis_hidden, vis_cot, rm_gain)
    visual_blocks = relayed_blocks(visual_grad, "tensor")
    handed = (
        jnp.dot(
            jnp.concatenate(visual_blocks, axis=0), bridge, preferred_element_type=jnp.float32
        )
        * reward_weight
    ).astype(jnp.bfloat16)

    parts = [[] for _ in range(count)]
    for g in range(groups):
        grads = attend(
            place_of, handed, (img_query, img_key, img_value), arrived[g], g, groups, count
        )
        parts[0].append(grads[0])
        for k in range(1, count):
            parts[k].append(
                lax.ppermute(grads[k], "tensor", [(i, (i - k) % count) for i in range(count)])
            )
    return tuple(place(place_of, parts, count))


def solution(mesh):
    placed = (
        P("dp", "tensor", None),
        P("dp", "tensor", None),
        P(),
        P("dp"),
        P("dp", "tensor"),
        P(None, "tensor"),
        P("dp", "tensor", None),
        P("dp", "tensor", None),
        P("dp", "tensor", None),
    )
    return jax.shard_map(
        local,
        mesh=mesh,
        in_specs=placed,
        out_specs=(P("dp", "tensor", None), P("dp", "tensor", None), P("dp", "tensor", None)),
        check_vma=False,
    )
```

```python
import functools

import jax
import jax.numpy as jnp
from jax import lax
from jax.experimental import pallas as pl
from jax.experimental.pallas import tpu as pltpu
from jax.sharding import PartitionSpec as P


HD = 128
GW = 64
GROUPS = 2


def norm_backward(hidden, cotangent, gain):
    hidden_f = hidden.astype(jnp.float32)
    scaled_cot = cotangent.astype(jnp.float32) * gain
    inv_rms = lax.rsqrt(jnp.mean(hidden_f * hidden_f, axis=-1, keepdims=True) + 1e-06)
    mixed = jnp.mean(hidden_f * scaled_cot, axis=-1, keepdims=True)
    return (inv_rms * scaled_cot - hidden_f * inv_rms * inv_rms * inv_rms * mixed).astype(
        jnp.bfloat16
    )


def total_over(value, axis):
    size = lax.axis_size(axis)
    if size & (size - 1):
        return lax.psum(value, axis)
    step = 1
    while step < size:
        value = value + lax.ppermute(value, axis, [(i, i ^ step) for i in range(size)])
        step *= 2
    return value


def relayed_blocks(block, axis):
    size = lax.axis_size(axis)
    here = lax.axis_index(axis)
    upward, downward = [], []
    up = down = block
    for step in range(size - 1):
        up = lax.ppermute(up, axis, [(i, i + 1) for i in range(step, size - 1)])
        down = lax.ppermute(down, axis, [(i + 1, i) for i in range(size - 1 - step)])
        upward.append(up)
        downward.append(down)
    return [block] + [
        jnp.where(here >= k, upward[k - 1], downward[size - k - 1]) for k in range(1, size)
    ]


def attend_kernel(count, scale, chunk, *refs):
    _, handed_ref, query_ref, key_ref, value_ref = refs[:5]
    blocks = refs[5 : 4 + count]
    outs = refs[4 + count : 4 + 2 * count]
    q_s, k_s, v_s, g_s, dq_s, dk_s, dv_s = refs[4 + 2 * count :]
    rows = query_ref.shape[1]
    length = rows * count
    seen = handed_ref.shape[0] // count
    q_s[pl.ds(0, rows)] = query_ref[0]
    k_s[pl.ds(0, rows)] = key_ref[0]
    v_s[pl.ds(0, rows)] = value_ref[0]
    for j, block in enumerate(blocks, 1):
        at = pl.ds(j * rows, rows)
        q_s[at] = block[0]
        k_s[at] = block[1]
        v_s[at] = block[2]
    token = lax.broadcasted_iota(jnp.int32, (rows, seen), 0)
    source = lax.broadcasted_iota(jnp.int32, (rows, seen), 1)
    spread = jnp.where(
        (token // (2 * GW)) * (GW // 2) + (token % GW) // 2 == source, 1.0, 0.0
    ).astype(jnp.bfloat16)
    for j in range(count):
        g_s[pl.ds(j * rows, rows)] = jnp.dot(
            spread, handed_ref[pl.ds(j * seen, seen)], preferred_element_type=jnp.float32
        ).astype(jnp.bfloat16)
    dk_s[...] = jnp.zeros_like(dk_s)
    dv_s[...] = jnp.zeros_like(dv_s)
    key_rows = k_s[...]
    value_rows = v_s[...]
    key_columns = key_rows.T
    both_last = (((1,), (1,)), ((), ()))

    def step(c, carry):
        at = pl.ds(pl.multiple_of(c * chunk, chunk), chunk)
        q = q_s[at]
        g = g_s[at]
        scores = lax.dot_general(key_rows, q, both_last, preferred_element_type=jnp.float32) * scale
        exp_scores = jnp.exp(scores - jnp.max(scores, axis=0, keepdims=True))
        weights = exp_scores * (1.0 / jnp.sum(exp_scores, axis=0, keepdims=True))
        grad_weights = lax.dot_general(value_rows, g, both_last, preferred_element_type=jnp.float32)
        row_dot = jnp.sum(weights * grad_weights, axis=0, keepdims=True)
        grad_scores = (weights * (grad_weights - row_dot)).astype(jnp.bfloat16)
        dv_s[...] += jnp.dot(weights.astype(jnp.bfloat16), g, preferred_element_type=jnp.float32)
        dk_s[...] += jnp.dot(grad_scores, q, preferred_element_type=jnp.float32)
        dq = jnp.dot(key_columns, grad_scores, preferred_element_type=jnp.float32)
        dq_s[at] = (dq * scale).T.astype(jnp.bfloat16)
        return carry

    lax.fori_loop(0, length // chunk, step, 0)
    for j, out in enumerate(outs):
        at = pl.ds(j * rows, rows)
        out[0] = dq_s[at]
        out[1] = (dk_s[at] * scale).astype(jnp.bfloat16)
        out[2] = dv_s[at].astype(jnp.bfloat16)


def attend(here, handed, own, blocks, group, groups, count):
    rows = own[0].shape[1]
    local_heads = handed.shape[1] // HD
    heads = local_heads // groups
    length = rows * count
    chunk = min(256, length)
    first = group * heads
    own_spec = pl.BlockSpec((1, rows, HD), lambda h, t: (0, 0, t[0] * local_heads + first + h))
    block_spec = pl.BlockSpec((3, rows, HD), lambda h, t: (0, 0, h))
    flops = 10 * heads * length * length * HD
    return pl.pallas_call(
        functools.partial(attend_kernel, count, HD**-0.5, chunk),
        grid_spec=pltpu.PrefetchScalarGridSpec(
            num_scalar_prefetch=1,
            grid=(heads,),
            in_specs=[pl.BlockSpec((handed.shape[0], HD), lambda h, t: (0, first + h))]
            + [own_spec] * 3
            + [block_spec] * (count - 1),
            out_specs=[block_spec] * count,
            scratch_shapes=[pltpu.VMEM((length, HD), jnp.bfloat16)] * 5
            + [pltpu.VMEM((length, HD), jnp.float32)] * 2,
        ),
        out_shape=[jax.ShapeDtypeStruct((3, rows, heads * HD), jnp.bfloat16)] * count,
        cost_estimate=pl.CostEstimate(
            flops=flops,
            bytes_accessed=12 * length * heads * HD,
            transcendentals=heads * length * length,
        ),
    )(here, handed, *own, *blocks)


def place_kernel(count, groups, *refs):
    parts = refs[1 : 1 + count * groups]
    outs = refs[1 + count * groups :]
    width = parts[0].shape[2]
    for k in range(count):

        @pl.when(pl.program_id(0) == k)
        def _():
            for g in range(groups):
                for i, out in enumerate(outs):
                    out[0, :, pl.ds(g * width, width)] = parts[k * groups + g][i]


def place(here, parts, count):
    groups = len(parts[0])
    rows, width = parts[0][0].shape[1:]
    flat = [part for ranked in parts for part in ranked]
    part_spec = pl.BlockSpec((3, rows, width), lambda k, t: (0, 0, 0))
    out_spec = pl.BlockSpec((1, rows, width * groups), lambda k, t: (0, 0, lax.rem(t[0] + k, count)))
    return pl.pallas_call(
        functools.partial(place_kernel, count, groups),
        grid_spec=pltpu.PrefetchScalarGridSpec(
            num_scalar_prefetch=1,
            grid=(count,),
            in_specs=[part_spec] * len(flat),
            out_specs=[out_spec] * 3,
        ),
        out_shape=[jax.ShapeDtypeStruct((1, rows, width * groups * count), jnp.bfloat16)] * 3,
        name="place",
    )(here, *flat)


def work(
    rm_hidden, rm_cotangent, rm_gain, rewards, visual_pos, bridge, img_query, img_key, img_value
):
    count = lax.axis_size("tensor")
    here = lax.axis_index("tensor")
    place_of = here[None].astype(jnp.int32)
    own_width = img_query.shape[2] // count
    groups = min(GROUPS, own_width // HD)
    width = own_width // groups

    def columns(array, k, g):
        first = lax.rem(here + k, count) * own_width + g * width
        return lax.dynamic_slice_in_dim(array[0], first, width, 1)

    arrived = []
    for g in range(groups):
        arrived.append(
            [
                lax.ppermute(
                    jnp.stack([columns(a, k, g) for a in (img_query, img_key, img_value)]),
                    "tensor",
                    [(i, (i + k) % count) for i in range(count)],
                )
                for k in range(1, count)
            ]
        )

    reward_sum = total_over(jnp.sum(rewards), "dp")
    sample_count = lax.axis_size("dp") * rewards.shape[0]
    reward_weight = rewards[0] * sample_count / reward_sum
    row_offset = here * rm_hidden.shape[1]
    local_rows = visual_pos[0] - row_offset
    vis_hidden = jnp.take(rm_hidden[0], local_rows, axis=0)
    vis_cot = jnp.take(rm_cotangent[0], local_rows, axis=0)
    visual_grad = norm_backward(vis_hidden, vis_cot, rm_gain)
    visual_blocks = relayed_blocks(visual_grad, "tensor")
    handed = (
        jnp.dot(
            jnp.concatenate(visual_blocks, axis=0), bridge, preferred_element_type=jnp.float32
        )
        * reward_weight
    ).astype(jnp.bfloat16)

    parts = [[] for _ in range(count)]
    for g in range(groups):
        grads = attend(
            place_of, handed, (img_query, img_key, img_value), arrived[g], g, groups, count
        )
        parts[0].append(grads[0])
        for k in range(1, count):
            parts[k].append(
                lax.ppermute(grads[k], "tensor", [(i, (i - k) % count) for i in range(count)])
            )
    return tuple(place(place_of, parts, count))


def solution(mesh):
    placed = (
        P("dp", "tensor", None),
        P("dp", "tensor", None),
        P(),
        P("dp"),
        P("dp", "tensor"),
        P(None, "tensor"),
        P("dp", "tensor", None),
        P("dp", "tensor", None),
        P("dp", "tensor", None),
    )
    return jax.shard_map(
        work,
        mesh=mesh,
        in_specs=placed,
        out_specs=(P("dp", "tensor", None), P("dp", "tensor", None), P("dp", "tensor", None)),
        check_vma=False,
    )
```

```python
import functools

import jax
import jax.numpy as jnp
from jax import lax
from jax.experimental import pallas as pl
from jax.experimental.pallas import tpu as pltpu
from jax.sharding import PartitionSpec as P


HD = 128
GW = 64


def norm_backward(hidden, cotangent, gain):
    hidden_f = hidden.astype(jnp.float32)
    scaled_cot = cotangent.astype(jnp.float32) * gain
    inv_rms = lax.rsqrt(jnp.mean(hidden_f * hidden_f, axis=-1, keepdims=True) + 1e-06)
    mixed = jnp.mean(hidden_f * scaled_cot, axis=-1, keepdims=True)
    return (inv_rms * scaled_cot - hidden_f * inv_rms * inv_rms * inv_rms * mixed).astype(
        jnp.bfloat16
    )


def head_groups(heads):
    return (1, 1, heads - 2) if heads > 2 else (heads,)


def total_over(value, axis):
    size = lax.axis_size(axis)
    if size & (size - 1):
        return lax.psum(value, axis)
    step = 1
    while step < size:
        value = value + lax.ppermute(value, axis, [(i, i ^ step) for i in range(size)])
        step *= 2
    return value


def relayed_blocks(block, axis):
    size = lax.axis_size(axis)
    here = lax.axis_index(axis)
    upward, downward = [], []
    up = down = block
    for step in range(size - 1):
        up = lax.ppermute(up, axis, [(i, i + 1) for i in range(step, size - 1)])
        down = lax.ppermute(down, axis, [(i + 1, i) for i in range(size - 1 - step)])
        upward.append(up)
        downward.append(down)
    return [block] + [
        jnp.where(here >= k, upward[k - 1], downward[size - k - 1]) for k in range(1, size)
    ]


def attend_kernel(count, scale, chunk, *refs):
    _, handed_ref, query_ref, key_ref, value_ref = refs[:5]
    blocks = refs[5 : 4 + count]
    outs = refs[4 + count : 4 + 2 * count]
    q_s, k_s, v_s, g_s, dq_s, dk_s, dv_s = refs[4 + 2 * count :]
    rows = query_ref.shape[1]
    length = rows * count
    seen = handed_ref.shape[0] // count
    q_s[pl.ds(0, rows)] = query_ref[0]
    k_s[pl.ds(0, rows)] = key_ref[0]
    v_s[pl.ds(0, rows)] = value_ref[0]
    for j, block in enumerate(blocks, 1):
        at = pl.ds(j * rows, rows)
        q_s[at] = block[0]
        k_s[at] = block[1]
        v_s[at] = block[2]
    token = lax.broadcasted_iota(jnp.int32, (rows, seen), 0)
    source = lax.broadcasted_iota(jnp.int32, (rows, seen), 1)
    spread = jnp.where(
        (token // (2 * GW)) * (GW // 2) + (token % GW) // 2 == source, 1.0, 0.0
    ).astype(jnp.bfloat16)
    for j in range(count):
        g_s[pl.ds(j * rows, rows)] = jnp.dot(
            spread, handed_ref[pl.ds(j * seen, seen)], preferred_element_type=jnp.float32
        ).astype(jnp.bfloat16)
    dk_s[...] = jnp.zeros_like(dk_s)
    dv_s[...] = jnp.zeros_like(dv_s)
    key_rows = k_s[...]
    value_rows = v_s[...]
    key_columns = key_rows.T
    both_last = (((1,), (1,)), ((), ()))

    def step(c, carry):
        at = pl.ds(pl.multiple_of(c * chunk, chunk), chunk)
        q = q_s[at]
        g = g_s[at]
        scores = lax.dot_general(key_rows, q, both_last, preferred_element_type=jnp.float32) * scale
        exp_scores = jnp.exp(scores - jnp.max(scores, axis=0, keepdims=True))
        weights = exp_scores * (1.0 / jnp.sum(exp_scores, axis=0, keepdims=True))
        grad_weights = lax.dot_general(value_rows, g, both_last, preferred_element_type=jnp.float32)
        row_dot = jnp.sum(weights * grad_weights, axis=0, keepdims=True)
        grad_scores = (weights * (grad_weights - row_dot)).astype(jnp.bfloat16)
        dv_s[...] += jnp.dot(weights.astype(jnp.bfloat16), g, preferred_element_type=jnp.float32)
        dk_s[...] += jnp.dot(grad_scores, q, preferred_element_type=jnp.float32)
        dq = jnp.dot(key_columns, grad_scores, preferred_element_type=jnp.float32)
        dq_s[at] = (dq * scale).T.astype(jnp.bfloat16)
        return carry

    lax.fori_loop(0, length // chunk, step, 0)
    for j, out in enumerate(outs):
        at = pl.ds(j * rows, rows)
        out[0] = dq_s[at]
        out[1] = (dk_s[at] * scale).astype(jnp.bfloat16)
        out[2] = dv_s[at].astype(jnp.bfloat16)


def attend(here, handed, own, blocks, first, heads, count):
    rows = own[0].shape[1]
    local_heads = handed.shape[1] // HD
    length = rows * count
    chunk = min(256, length)
    own_spec = pl.BlockSpec((1, rows, HD), lambda h, t: (0, 0, t[0] * local_heads + first + h))
    block_spec = pl.BlockSpec((3, rows, HD), lambda h, t: (0, 0, h))
    flops = 10 * heads * length * length * HD
    return pl.pallas_call(
        functools.partial(attend_kernel, count, HD**-0.5, chunk),
        grid_spec=pltpu.PrefetchScalarGridSpec(
            num_scalar_prefetch=1,
            grid=(heads,),
            in_specs=[pl.BlockSpec((handed.shape[0], HD), lambda h, t: (0, first + h))]
            + [own_spec] * 3
            + [block_spec] * (count - 1),
            out_specs=[block_spec] * count,
            scratch_shapes=[pltpu.VMEM((length, HD), jnp.bfloat16)] * 5
            + [pltpu.VMEM((length, HD), jnp.float32)] * 2,
        ),
        out_shape=[jax.ShapeDtypeStruct((3, rows, heads * HD), jnp.bfloat16)] * count,
        cost_estimate=pl.CostEstimate(
            flops=flops,
            bytes_accessed=12 * length * heads * HD,
            transcendentals=heads * length * length,
        ),
    )(here, handed, *own, *blocks)


def place_kernel(count, first, *refs):
    here = refs[0][0]
    parts = refs[1 : 1 + count]
    outs = refs[-4:-1]
    sems = refs[-1]
    width = parts[0].shape[2]
    own_width = outs[0].shape[2] // count
    copies = []
    for k, part in enumerate(parts):
        column = pl.multiple_of(lax.rem(here + k, count) * own_width + first, HD)
        for i, out in enumerate(outs):
            copies.append(
                pltpu.make_async_copy(
                    part.at[i], out.at[0, :, pl.ds(column, width)], sems.at[3 * k + i]
                )
            )
    for copy in copies:
        copy.start()
    for copy in copies:
        copy.wait()


def place(here, parts, outs, shape, first):
    count = len(parts)
    anywhere = pl.BlockSpec(memory_space=pl.ANY)
    held = len(outs)
    return pl.pallas_call(
        functools.partial(place_kernel, count, first),
        in_specs=[pl.BlockSpec(memory_space=pltpu.SMEM)]
        + [pl.BlockSpec(memory_space=pltpu.VMEM)] * count
        + [anywhere] * held,
        out_specs=[anywhere] * 3,
        out_shape=[jax.ShapeDtypeStruct(shape, jnp.bfloat16)] * 3,
        input_output_aliases={1 + count + i: i for i in range(held)},
        scratch_shapes=[pltpu.SemaphoreType.DMA((3 * count,))],
        cost_estimate=pl.CostEstimate(
            flops=0, bytes_accessed=4 * count * parts[0].size, transcendentals=0
        ),
    )(here, *parts, *outs)


def work(
    rm_hidden, rm_cotangent, rm_gain, rewards, visual_pos, bridge, img_query, img_key, img_value
):
    count = lax.axis_size("tensor")
    here = lax.axis_index("tensor")
    place_of = here[None].astype(jnp.int32)
    own_width = img_query.shape[2] // count
    groups = head_groups(own_width // HD)
    starts = [sum(groups[:g]) for g in range(len(groups))]

    def columns(array, k, g):
        first = lax.rem(here + k, count) * own_width + starts[g] * HD
        return lax.dynamic_slice_in_dim(array[0], first, groups[g] * HD, 1)

    arrived = []
    for g in range(len(groups)):
        arrived.append(
            [
                lax.ppermute(
                    jnp.stack([columns(a, k, g) for a in (img_query, img_key, img_value)]),
                    "tensor",
                    [(i, (i + k) % count) for i in range(count)],
                )
                for k in range(1, count)
            ]
        )

    reward_sum = total_over(jnp.sum(rewards), "dp")
    sample_count = lax.axis_size("dp") * rewards.shape[0]
    reward_weight = rewards[0] * sample_count / reward_sum
    row_offset = here * rm_hidden.shape[1]
    local_rows = visual_pos[0] - row_offset
    vis_hidden = jnp.take(rm_hidden[0], local_rows, axis=0)
    vis_cot = jnp.take(rm_cotangent[0], local_rows, axis=0)
    visual_grad = norm_backward(vis_hidden, vis_cot, rm_gain)
    visual_blocks = relayed_blocks(visual_grad, "tensor")
    handed = (
        jnp.dot(
            jnp.concatenate(visual_blocks, axis=0), bridge, preferred_element_type=jnp.float32
        )
        * reward_weight
    ).astype(jnp.bfloat16)

    outs = ()
    for g, heads in enumerate(groups):
        grads = attend(
            place_of, handed, (img_query, img_key, img_value), arrived[g], starts[g], heads, count
        )
        parts = [grads[0]] + [
            lax.ppermute(grads[k], "tensor", [(i, (i - k) % count) for i in range(count)])
            for k in range(1, count)
        ]
        outs = place(place_of, parts, outs, img_query.shape, starts[g] * HD)
    return tuple(outs)


def solution(mesh):
    placed = (
        P("dp", "tensor", None),
        P("dp", "tensor", None),
        P(),
        P("dp"),
        P("dp", "tensor"),
        P(None, "tensor"),
        P("dp", "tensor", None),
        P("dp", "tensor", None),
        P("dp", "tensor", None),
    )
    return jax.shard_map(
        work,
        mesh=mesh,
        in_specs=placed,
        out_specs=(P("dp", "tensor", None), P("dp", "tensor", None), P("dp", "tensor", None)),
        check_vma=False,
    )
```

```python
import functools

import jax
import jax.numpy as jnp
from jax import lax
from jax.experimental import pallas as pl
from jax.experimental.pallas import tpu as pltpu
from jax.sharding import PartitionSpec as P


HD = 128
GW = 64
IN_HEADS = (2, 2)
OUT_HEADS = (2, 1, 1)


def visual_kernel(here_ref, pos_ref, hidden_ref, cot_ref, gain_ref, out_ref):
    rows = hidden_ref.shape[1]
    picked = out_ref.shape[0]
    row = lax.broadcasted_iota(jnp.int32, (rows, picked), 0) + here_ref[0] * rows
    pick = jnp.where(row == pos_ref[...], 1.0, 0.0).astype(jnp.bfloat16)
    first_both = (((0,), (0,)), ((), ()))
    hidden = lax.dot_general(pick, hidden_ref[0], first_both, preferred_element_type=jnp.float32)
    cot = lax.dot_general(pick, cot_ref[0], first_both, preferred_element_type=jnp.float32)
    scaled_cot = cot * gain_ref[...]
    inv_rms = lax.rsqrt(jnp.mean(hidden * hidden, axis=-1, keepdims=True) + 1e-06)
    mixed = jnp.mean(hidden * scaled_cot, axis=-1, keepdims=True)
    out_ref[...] = (inv_rms * scaled_cot - hidden * (inv_rms * inv_rms * inv_rms * mixed)).astype(
        jnp.bfloat16
    )


def visual_grads(here, positions, hidden, cotangent, gain):
    picked, depth = positions.shape[1], hidden.shape[2]
    vmem = pl.BlockSpec(memory_space=pltpu.VMEM)
    return pl.pallas_call(
        visual_kernel,
        in_specs=[pl.BlockSpec(memory_space=pltpu.SMEM)] + [vmem] * 4,
        out_specs=vmem,
        out_shape=jax.ShapeDtypeStruct((picked, depth), jnp.bfloat16),
        cost_estimate=pl.CostEstimate(
            flops=4 * picked * hidden.size, bytes_accessed=4 * hidden.size, transcendentals=0
        ),
        name="visual",
    )(here, positions, hidden, cotangent, gain[None])


def pack_kernel(count, first, here_ref, *refs):
    sources, outs, sems = refs[:3], refs[3:-1], refs[-1]
    width = outs[0].shape[2]
    own_width = sources[0].shape[2] // count
    copies = []
    for k, out in enumerate(outs, 1):
        column = pl.multiple_of((here_ref[0] ^ k) * own_width + first, HD)
        for i, source in enumerate(sources):
            copies.append(
                pltpu.make_async_copy(
                    source.at[0, :, pl.ds(column, width)], out.at[i], sems.at[3 * k - 3 + i]
                )
            )
    for copy in copies:
        copy.start()
    for copy in copies:
        copy.wait()


def pack(here, sources, first, width, count):
    rows = sources[0].shape[1]
    return pl.pallas_call(
        functools.partial(pack_kernel, count, first),
        in_specs=[pl.BlockSpec(memory_space=pltpu.SMEM)]
        + [pl.BlockSpec(memory_space=pl.ANY)] * 3,
        out_specs=[pl.BlockSpec(memory_space=pltpu.VMEM)] * (count - 1),
        out_shape=[jax.ShapeDtypeStruct((3, rows, width), jnp.bfloat16)] * (count - 1),
        scratch_shapes=[pltpu.SemaphoreType.DMA((3 * count - 3,))],
        cost_estimate=pl.CostEstimate(
            flops=0, bytes_accessed=12 * count * rows * width, transcendentals=0
        ),
    )(here, *sources)


def split(heads, parts):
    return parts if sum(parts) == heads else (heads,)


def partners(size, k):
    return [(i, i ^ k) for i in range(size)]


def total_over(value, axis):
    size = lax.axis_size(axis)
    step = 1
    while step < size:
        value = value + lax.ppermute(value, axis, partners(size, step))
        step *= 2
    return value


def gathered(block, axis):
    size = lax.axis_size(axis)
    held = {0: block}
    step = size // 2
    while step:
        for k in sorted(held):
            held[k ^ step] = lax.ppermute(held[k], axis, partners(size, step))
        step //= 2
    return [held[k] for k in range(size)]


def attend_kernel(count, scale, chunk, *refs):
    _, handed_ref, query_ref, key_ref, value_ref = refs[:5]
    blocks = refs[5 : 4 + count]
    outs = refs[4 + count : 4 + 2 * count]
    q_s, k_s, v_s, g_s, dq_s, dk_s, dv_s = refs[4 + 2 * count :]
    rows = query_ref.shape[1]
    length = rows * count
    seen = handed_ref.shape[0] // count
    q_s[pl.ds(0, rows)] = query_ref[0]
    k_s[pl.ds(0, rows)] = key_ref[0]
    v_s[pl.ds(0, rows)] = value_ref[0]
    for j, block in enumerate(blocks, 1):
        at = pl.ds(j * rows, rows)
        q_s[at] = block[0]
        k_s[at] = block[1]
        v_s[at] = block[2]
    token = lax.broadcasted_iota(jnp.int32, (rows, seen), 0)
    source = lax.broadcasted_iota(jnp.int32, (rows, seen), 1)
    spread = jnp.where(
        (token // (2 * GW)) * (GW // 2) + (token % GW) // 2 == source, 1.0, 0.0
    ).astype(jnp.bfloat16)
    for j in range(count):
        g_s[pl.ds(j * rows, rows)] = jnp.dot(
            spread, handed_ref[pl.ds(j * seen, seen)], preferred_element_type=jnp.float32
        ).astype(jnp.bfloat16)
    dk_s[...] = jnp.zeros_like(dk_s)
    dv_s[...] = jnp.zeros_like(dv_s)
    key_rows = k_s[...]
    value_rows = v_s[...]
    key_columns = key_rows.T
    both_last = (((1,), (1,)), ((), ()))

    def step(c, carry):
        at = pl.ds(pl.multiple_of(c * chunk, chunk), chunk)
        q = q_s[at]
        g = g_s[at]
        scores = lax.dot_general(key_rows, q, both_last, preferred_element_type=jnp.float32) * scale
        exp_scores = jnp.exp(scores - jnp.max(scores, axis=0, keepdims=True))
        weights = exp_scores * (1.0 / jnp.sum(exp_scores, axis=0, keepdims=True))
        grad_weights = lax.dot_general(value_rows, g, both_last, preferred_element_type=jnp.float32)
        row_dot = jnp.sum(weights * grad_weights, axis=0, keepdims=True)
        grad_scores = (weights * (grad_weights - row_dot)).astype(jnp.bfloat16)
        dv_s[...] += jnp.dot(weights.astype(jnp.bfloat16), g, preferred_element_type=jnp.float32)
        dk_s[...] += jnp.dot(grad_scores, q, preferred_element_type=jnp.float32)
        dq = jnp.dot(key_columns, grad_scores, preferred_element_type=jnp.float32)
        dq_s[at] = (dq * scale).T.astype(jnp.bfloat16)
        return carry

    lax.fori_loop(0, length // chunk, step, 0)
    for j, out in enumerate(outs):
        at = pl.ds(j * rows, rows)
        out[0] = dq_s[at]
        out[1] = (dk_s[at] * scale).astype(jnp.bfloat16)
        out[2] = dv_s[at].astype(jnp.bfloat16)


def attend(here, handed, own, blocks, first, skip, heads, count):
    rows = own[0].shape[1]
    local_heads = handed.shape[1] // HD
    length = rows * count
    chunk = min(256, length)
    own_spec = pl.BlockSpec((1, rows, HD), lambda h, t: (0, 0, t[0] * local_heads + first + h))
    out_spec = pl.BlockSpec((3, rows, HD), lambda h, t: (0, 0, h))
    block_spec = pl.BlockSpec((3, rows, HD), lambda h, t: (0, 0, skip + h))
    flops = 10 * heads * length * length * HD
    return pl.pallas_call(
        functools.partial(attend_kernel, count, HD**-0.5, chunk),
        grid_spec=pltpu.PrefetchScalarGridSpec(
            num_scalar_prefetch=1,
            grid=(heads,),
            in_specs=[pl.BlockSpec((handed.shape[0], HD), lambda h, t: (0, first + h))]
            + [own_spec] * 3
            + [block_spec] * (count - 1),
            out_specs=[out_spec] * count,
            scratch_shapes=[pltpu.VMEM((length, HD), jnp.bfloat16)] * 5
            + [pltpu.VMEM((length, HD), jnp.float32)] * 2,
        ),
        out_shape=[jax.ShapeDtypeStruct((3, rows, heads * HD), jnp.bfloat16)] * count,
        cost_estimate=pl.CostEstimate(
            flops=flops,
            bytes_accessed=12 * length * heads * HD,
            transcendentals=heads * length * length,
        ),
    )(here, handed, *own, *blocks)


def place_kernel(count, first, *refs):
    here = refs[0][0]
    parts = refs[1 : 1 + count]
    outs = refs[-4:-1]
    sems = refs[-1]
    width = parts[0].shape[2]
    own_width = outs[0].shape[2] // count
    copies = []
    for k, part in enumerate(parts):
        column = pl.multiple_of((here ^ k) * own_width + first, HD)
        for i, out in enumerate(outs):
            copies.append(
                pltpu.make_async_copy(
                    part.at[i], out.at[0, :, pl.ds(column, width)], sems.at[3 * k + i]
                )
            )
    for copy in copies:
        copy.start()
    for copy in copies:
        copy.wait()


def place(here, parts, outs, shape, first):
    count = len(parts)
    anywhere = pl.BlockSpec(memory_space=pl.ANY)
    held = len(outs)
    return pl.pallas_call(
        functools.partial(place_kernel, count, first),
        in_specs=[pl.BlockSpec(memory_space=pltpu.SMEM)]
        + [pl.BlockSpec(memory_space=pltpu.VMEM)] * count
        + [anywhere] * held,
        out_specs=[anywhere] * 3,
        out_shape=[jax.ShapeDtypeStruct(shape, jnp.bfloat16)] * 3,
        input_output_aliases={1 + count + i: i for i in range(held)},
        scratch_shapes=[pltpu.SemaphoreType.DMA((3 * count,))],
        cost_estimate=pl.CostEstimate(
            flops=0, bytes_accessed=4 * count * parts[0].size, transcendentals=0
        ),
    )(here, *parts, *outs)


def work(
    rm_hidden, rm_cotangent, rm_gain, rewards, visual_pos, bridge, img_query, img_key, img_value
):
    count = lax.axis_size("tensor")
    here = lax.axis_index("tensor")
    place_of = here[None].astype(jnp.int32)
    own_width = img_query.shape[2] // count
    own = (img_query, img_key, img_value)
    visual_grad = visual_grads(place_of, visual_pos, rm_hidden, rm_cotangent, rm_gain)
    visual_blocks = gathered(visual_grad, "tensor")

    arrived = []
    for heads in split(own_width // HD, IN_HEADS):
        packed = pack(place_of, own, len(arrived) * HD, heads * HD, count)
        blocks = [
            lax.ppermute(packed[k - 1], "tensor", partners(count, k))
            for k in range(1, count)
        ]
        arrived += [(blocks, skip) for skip in range(heads)]

    reward_sum = total_over(jnp.sum(rewards), "dp")
    sample_count = lax.axis_size("dp") * rewards.shape[0]
    reward_weight = rewards[0] * sample_count / reward_sum
    handed = (
        jnp.dot(
            jnp.concatenate(visual_blocks, axis=0), bridge, preferred_element_type=jnp.float32
        )
        * reward_weight
    ).astype(jnp.bfloat16)

    outs = ()
    first = 0
    for heads in split(own_width // HD, OUT_HEADS):
        blocks, skip = arrived[first]
        grads = attend(place_of, handed, own, blocks, first, skip, heads, count)
        parts = [grads[0]] + [
            lax.ppermute(grads[k], "tensor", partners(count, k)) for k in range(1, count)
        ]
        outs = place(place_of, parts, outs, img_query.shape, first * HD)
        first += heads
    return tuple(outs)


def solution(mesh):
    placed = (
        P("dp", "tensor", None),
        P("dp", "tensor", None),
        P(),
        P("dp"),
        P("dp", "tensor"),
        P(None, "tensor"),
        P("dp", "tensor", None),
        P("dp", "tensor", None),
        P("dp", "tensor", None),
    )
    return jax.shard_map(
        work,
        mesh=mesh,
        in_specs=placed,
        out_specs=(P("dp", "tensor", None), P("dp", "tensor", None), P("dp", "tensor", None)),
        check_vma=False,
    )
```

```python
import functools

import jax
import jax.numpy as jnp
from jax import lax
from jax.experimental import pallas as pl
from jax.experimental.pallas import tpu as pltpu
from jax.sharding import PartitionSpec as P


HD = 128
GW = 64
IN_HEADS = (2, 2)
OUT_HEADS = (2, 1, 1)


def visual_kernel(here_ref, pos_ref, hidden_ref, cot_ref, gain_ref, out_ref):
    rows = hidden_ref.shape[1]
    picked = out_ref.shape[0]
    row = lax.broadcasted_iota(jnp.int32, (rows, picked), 0) + here_ref[0] * rows
    pick = jnp.where(row == pos_ref[...], 1.0, 0.0).astype(jnp.bfloat16)
    first_both = (((0,), (0,)), ((), ()))
    hidden = lax.dot_general(pick, hidden_ref[0], first_both, preferred_element_type=jnp.float32)
    cot = lax.dot_general(pick, cot_ref[0], first_both, preferred_element_type=jnp.float32)
    lanes = gain_ref.shape[1]
    scaled_cot = jnp.concatenate(
        [
            cot[:, j * lanes : (j + 1) * lanes] * gain_ref[pl.ds(j, 1)]
            for j in range(gain_ref.shape[0])
        ],
        axis=1,
    )
    inv_rms = lax.rsqrt(jnp.mean(hidden * hidden, axis=-1, keepdims=True) + 1e-06)
    mixed = jnp.mean(hidden * scaled_cot, axis=-1, keepdims=True)
    out_ref[...] = (inv_rms * scaled_cot - hidden * (inv_rms * inv_rms * inv_rms * mixed)).astype(
        jnp.bfloat16
    )


def visual_grads(here, positions, hidden, cotangent, gain):
    picked, depth = positions.shape[1], hidden.shape[2]
    vmem = pl.BlockSpec(memory_space=pltpu.VMEM)
    return pl.pallas_call(
        visual_kernel,
        in_specs=[pl.BlockSpec(memory_space=pltpu.SMEM)] + [vmem] * 4,
        out_specs=vmem,
        out_shape=jax.ShapeDtypeStruct((picked, depth), jnp.bfloat16),
        cost_estimate=pl.CostEstimate(
            flops=4 * picked * hidden.size, bytes_accessed=4 * hidden.size, transcendentals=0
        ),
        compiler_params=pltpu.CompilerParams(vmem_limit_bytes=(8 << 20) + 12 * hidden.size),
        name="visual",
    )(here, positions, hidden, cotangent, gain.reshape(-1, HD))


def pack_kernel(count, first, here_ref, *refs):
    sources, outs, sems = refs[:3], refs[3:-1], refs[-1]
    width = outs[0].shape[2]
    own_width = sources[0].shape[2] // count
    copies = []
    for k, out in enumerate(outs):
        column = pl.multiple_of((here_ref[0] ^ k) * own_width + first, HD)
        for i, source in enumerate(sources):
            copies.append(
                pltpu.make_async_copy(
                    source.at[0, :, pl.ds(column, width)], out.at[i], sems.at[3 * k + i]
                )
            )
    for copy in copies:
        copy.start()
    for copy in copies:
        copy.wait()


def pack(here, sources, first, width, count):
    rows = sources[0].shape[1]
    return pl.pallas_call(
        functools.partial(pack_kernel, count, first),
        in_specs=[pl.BlockSpec(memory_space=pltpu.SMEM)]
        + [pl.BlockSpec(memory_space=pl.ANY)] * 3,
        out_specs=[pl.BlockSpec(memory_space=pltpu.VMEM)] * count,
        out_shape=[jax.ShapeDtypeStruct((3, rows, width), jnp.bfloat16)] * count,
        scratch_shapes=[pltpu.SemaphoreType.DMA((3 * count,))],
        cost_estimate=pl.CostEstimate(
            flops=0, bytes_accessed=12 * count * rows * width, transcendentals=0
        ),
        compiler_params=pltpu.CompilerParams(
            vmem_limit_bytes=(1 << 20) + 6 * count * rows * width
        ),
    )(here, *sources)


def split(heads, parts):
    return parts if sum(parts) == heads else (heads,)


def partners(size, k):
    return [(i, i ^ k) for i in range(size)]


def total_over(value, axis):
    size = lax.axis_size(axis)
    step = 1
    while step < size:
        value = value + lax.ppermute(value, axis, partners(size, step))
        step *= 2
    return value


def gathered(block, axis):
    size = lax.axis_size(axis)
    held = {0: block}
    step = size // 2
    while step:
        for k in sorted(held):
            held[k ^ step] = lax.ppermute(held[k], axis, partners(size, step))
        step //= 2
    return [held[k] for k in range(size)]


def attend_kernel(count, scale, chunk, *refs):
    handed_ref = refs[0]
    blocks = refs[1 : 1 + count]
    outs = refs[1 + count : 1 + 2 * count]
    q_s, k_s, v_s, g_s, dq_s, dk_s, dv_s = refs[1 + 2 * count :]
    rows = blocks[0].shape[1]
    length = rows * count
    seen = handed_ref.shape[0] // count
    for j, block in enumerate(blocks):
        at = pl.ds(j * rows, rows)
        q_s[at] = block[0]
        k_s[at] = block[1]
        v_s[at] = block[2]
    token = lax.broadcasted_iota(jnp.int32, (rows, seen), 0)
    source = lax.broadcasted_iota(jnp.int32, (rows, seen), 1)
    spread = jnp.where(
        (token // (2 * GW)) * (GW // 2) + (token % GW) // 2 == source, 1.0, 0.0
    ).astype(jnp.bfloat16)
    for j in range(count):
        g_s[pl.ds(j * rows, rows)] = jnp.dot(
            spread, handed_ref[pl.ds(j * seen, seen)], preferred_element_type=jnp.float32
        ).astype(jnp.bfloat16)
    dk_s[...] = jnp.zeros_like(dk_s)
    dv_s[...] = jnp.zeros_like(dv_s)
    key_rows = k_s[...]
    value_rows = v_s[...]
    key_columns = key_rows.T
    both_last = (((1,), (1,)), ((), ()))

    def step(c, carry):
        at = pl.ds(pl.multiple_of(c * chunk, chunk), chunk)
        q = q_s[at]
        g = g_s[at]
        scores = lax.dot_general(key_rows, q, both_last, preferred_element_type=jnp.float32) * scale
        exp_scores = jnp.exp(scores - jnp.max(scores, axis=0, keepdims=True))
        weights = exp_scores * (1.0 / jnp.sum(exp_scores, axis=0, keepdims=True))
        grad_weights = lax.dot_general(value_rows, g, both_last, preferred_element_type=jnp.float32)
        row_dot = jnp.sum(weights * grad_weights, axis=0, keepdims=True)
        grad_scores = (weights * (grad_weights - row_dot)).astype(jnp.bfloat16)
        dv_s[...] += jnp.dot(weights.astype(jnp.bfloat16), g, preferred_element_type=jnp.float32)
        dk_s[...] += jnp.dot(grad_scores, q, preferred_element_type=jnp.float32)
        dq = jnp.dot(key_columns, grad_scores, preferred_element_type=jnp.float32)
        dq_s[at] = (dq * scale).T.astype(jnp.bfloat16)
        return carry

    lax.fori_loop(0, length // chunk, step, 0)
    for j, out in enumerate(outs):
        at = pl.ds(j * rows, rows)
        out[0] = dq_s[at]
        out[1] = (dk_s[at] * scale).astype(jnp.bfloat16)
        out[2] = dv_s[at].astype(jnp.bfloat16)


def attend(handed, blocks, first, skip, heads):
    count = len(blocks)
    rows = blocks[0].shape[1]
    length = rows * count
    chunk = min(256, length)
    out_spec = pl.BlockSpec((3, rows, HD), lambda h: (0, 0, h))
    block_spec = pl.BlockSpec((3, rows, HD), lambda h: (0, 0, skip + h))
    return pl.pallas_call(
        functools.partial(attend_kernel, count, HD**-0.5, chunk),
        grid=(heads,),
        in_specs=[pl.BlockSpec((handed.shape[0], HD), lambda h: (0, first + h))]
        + [block_spec] * count,
        out_specs=[out_spec] * count,
        scratch_shapes=[pltpu.VMEM((length, HD), jnp.bfloat16)] * 5
        + [pltpu.VMEM((length, HD), jnp.float32)] * 2,
        out_shape=[jax.ShapeDtypeStruct((3, rows, heads * HD), jnp.bfloat16)] * count,
        cost_estimate=pl.CostEstimate(
            flops=10 * heads * length * length * HD,
            bytes_accessed=12 * length * heads * HD,
            transcendentals=heads * length * length,
        ),
        compiler_params=pltpu.CompilerParams(
            vmem_limit_bytes=(4 << 20) + 48 * length * chunk
        ),
    )(handed, *blocks)


def place_kernel(count, first, *refs):
    here = refs[0][0]
    parts = refs[1 : 1 + count]
    outs = refs[-4:-1]
    sems = refs[-1]
    width = parts[0].shape[2]
    own_width = outs[0].shape[2] // count
    copies = []
    for k, part in enumerate(parts):
        column = pl.multiple_of((here ^ k) * own_width + first, HD)
        for i, out in enumerate(outs):
            copies.append(
                pltpu.make_async_copy(
                    part.at[i], out.at[0, :, pl.ds(column, width)], sems.at[3 * k + i]
                )
            )
    for copy in copies:
        copy.start()
    for copy in copies:
        copy.wait()


def place(here, parts, outs, shape, first):
    count = len(parts)
    anywhere = pl.BlockSpec(memory_space=pl.ANY)
    held = len(outs)
    return pl.pallas_call(
        functools.partial(place_kernel, count, first),
        in_specs=[pl.BlockSpec(memory_space=pltpu.SMEM)]
        + [pl.BlockSpec(memory_space=pltpu.VMEM)] * count
        + [anywhere] * held,
        out_specs=[anywhere] * 3,
        out_shape=[jax.ShapeDtypeStruct(shape, jnp.bfloat16)] * 3,
        input_output_aliases={1 + count + i: i for i in range(held)},
        scratch_shapes=[pltpu.SemaphoreType.DMA((3 * count,))],
        cost_estimate=pl.CostEstimate(
            flops=0, bytes_accessed=4 * count * parts[0].size, transcendentals=0
        ),
        compiler_params=pltpu.CompilerParams(
            vmem_limit_bytes=(1 << 20) + 2 * count * parts[0].size
        ),
    )(here, *parts, *outs)


def work(
    rm_hidden, rm_cotangent, rm_gain, rewards, visual_pos, bridge, img_query, img_key, img_value
):
    count = lax.axis_size("tensor")
    here = lax.axis_index("tensor")
    place_of = here[None].astype(jnp.int32)
    own_width = img_query.shape[2] // count
    own = (img_query, img_key, img_value)
    visual_grad = visual_grads(place_of, visual_pos, rm_hidden, rm_cotangent, rm_gain)
    visual_blocks = gathered(visual_grad, "tensor")

    arrived = []
    for heads in split(own_width // HD, IN_HEADS):
        packed = pack(place_of, own, len(arrived) * HD, heads * HD, count)
        blocks = [packed[0]] + [
            lax.ppermute(packed[k], "tensor", partners(count, k)) for k in range(1, count)
        ]
        arrived += [(blocks, skip) for skip in range(heads)]

    reward_sum = total_over(jnp.sum(rewards), "dp")
    sample_count = lax.axis_size("dp") * rewards.shape[0]
    reward_weight = rewards[0] * sample_count / reward_sum
    handed = (
        jnp.dot(
            jnp.concatenate(visual_blocks, axis=0), bridge, preferred_element_type=jnp.float32
        )
        * reward_weight
    ).astype(jnp.bfloat16)

    outs = ()
    first = 0
    for heads in split(own_width // HD, OUT_HEADS):
        blocks, skip = arrived[first]
        grads = attend(handed, blocks, first, skip, heads)
        parts = [grads[0]] + [
            lax.ppermute(grads[k], "tensor", partners(count, k)) for k in range(1, count)
        ]
        outs = place(place_of, parts, outs, img_query.shape, first * HD)
        first += heads
    return tuple(outs)


def solution(mesh):
    placed = (
        P("dp", "tensor", None),
        P("dp", "tensor", None),
        P(),
        P("dp"),
        P("dp", "tensor"),
        P(None, "tensor"),
        P("dp", "tensor", None),
        P("dp", "tensor", None),
        P("dp", "tensor", None),
    )
    return jax.shard_map(
        work,
        mesh=mesh,
        in_specs=placed,
        out_specs=(P("dp", "tensor", None), P("dp", "tensor", None), P("dp", "tensor", None)),
        check_vma=False,
    )
```

```python
import functools

import jax
import jax.numpy as jnp
from jax import lax
from jax.experimental import pallas as pl
from jax.experimental.pallas import tpu as pltpu
from jax.sharding import PartitionSpec as P


HD = 128
GW = 64
IN_HEADS = (2, 1, 1)
OUT_HEADS = (2, 1, 1)


def in_hbm(array):
    return pltpu.with_memory_space_constraint(array, pltpu.HBM)


def visual_kernel(here_ref, pos_ref, gain_ref, hidden_hbm, cot_hbm, out_ref, held, sems):
    rows = hidden_hbm.shape[1]
    picked = out_ref.shape[0]
    pieces = sems.shape[1]
    piece = rows // pieces
    copies = []
    for i, source in enumerate((hidden_hbm, cot_hbm)):
        for j in range(pieces):
            at = pl.ds(j * piece, piece)
            copies.append(
                pltpu.make_async_copy(source.at[0, at], held.at[i, at], sems.at[i, j])
            )
    for copy in copies:
        copy.start()
    row = lax.broadcasted_iota(jnp.int32, (rows, picked), 0) + here_ref[0] * rows
    pick = jnp.where(row == pos_ref[...], 1.0, 0.0).astype(jnp.bfloat16)
    first_both = (((0,), (0,)), ((), ()))
    for copy in copies:
        copy.wait()
    hidden = lax.dot_general(pick, held[0], first_both, preferred_element_type=jnp.float32)
    cot = lax.dot_general(pick, held[1], first_both, preferred_element_type=jnp.float32)
    lanes = gain_ref.shape[1]
    scaled_cot = jnp.concatenate(
        [
            cot[:, j * lanes : (j + 1) * lanes] * gain_ref[pl.ds(j, 1)]
            for j in range(gain_ref.shape[0])
        ],
        axis=1,
    )
    inv_rms = lax.rsqrt(jnp.mean(hidden * hidden, axis=-1, keepdims=True) + 1e-06)
    mixed = jnp.mean(hidden * scaled_cot, axis=-1, keepdims=True)
    out_ref[...] = (inv_rms * scaled_cot - hidden * (inv_rms * inv_rms * inv_rms * mixed)).astype(
        jnp.bfloat16
    )


def visual_grads(here, positions, hidden, cotangent, gain):
    picked, depth = positions.shape[1], hidden.shape[2]
    rows = hidden.shape[1]
    pieces = 8 if rows % 64 == 0 else 1
    vmem = pl.BlockSpec(memory_space=pltpu.VMEM)
    hbm = pl.BlockSpec(memory_space=pltpu.HBM)
    return pl.pallas_call(
        visual_kernel,
        in_specs=[pl.BlockSpec(memory_space=pltpu.SMEM), vmem, vmem, hbm, hbm],
        out_specs=vmem,
        scratch_shapes=[
            pltpu.VMEM((2, rows, depth), jnp.bfloat16),
            pltpu.SemaphoreType.DMA((2, pieces)),
        ],
        out_shape=jax.ShapeDtypeStruct((picked, depth), jnp.bfloat16),
        cost_estimate=pl.CostEstimate(
            flops=4 * picked * hidden.size, bytes_accessed=4 * hidden.size, transcendentals=0
        ),
        compiler_params=pltpu.CompilerParams(vmem_limit_bytes=(8 << 20) + 12 * hidden.size),
        name="visual",
    )(here, positions, gain.reshape(-1, HD), in_hbm(hidden), in_hbm(cotangent))


def pack_kernel(count, first, here_ref, *refs):
    sources, outs, sems = refs[:3], refs[3:-1], refs[-1]
    width = outs[0].shape[2]
    own_width = sources[0].shape[2] // count
    copies = []
    for k, out in enumerate(outs):
        column = pl.multiple_of((here_ref[0] ^ k) * own_width + first, HD)
        for i, source in enumerate(sources):
            copies.append(
                pltpu.make_async_copy(
                    source.at[0, :, pl.ds(column, width)], out.at[i], sems.at[3 * k + i]
                )
            )
    for copy in copies:
        copy.start()
    for copy in copies:
        copy.wait()


def pack(here, sources, first, width, count):
    rows = sources[0].shape[1]
    return pl.pallas_call(
        functools.partial(pack_kernel, count, first),
        in_specs=[pl.BlockSpec(memory_space=pltpu.SMEM)]
        + [pl.BlockSpec(memory_space=pltpu.HBM)] * 3,
        out_specs=[pl.BlockSpec(memory_space=pltpu.VMEM)] * count,
        out_shape=[jax.ShapeDtypeStruct((3, rows, width), jnp.bfloat16)] * count,
        scratch_shapes=[pltpu.SemaphoreType.DMA((3 * count,))],
        cost_estimate=pl.CostEstimate(
            flops=0, bytes_accessed=12 * count * rows * width, transcendentals=0
        ),
        compiler_params=pltpu.CompilerParams(
            vmem_limit_bytes=(1 << 20) + 6 * count * rows * width
        ),
    )(here, *map(in_hbm, sources))


def split(heads, parts):
    return parts if sum(parts) == heads else (heads,)


def partners(size, k):
    return [(i, i ^ k) for i in range(size)]


def total_over(value, axis):
    size = lax.axis_size(axis)
    step = 1
    while step < size:
        value = value + lax.ppermute(value, axis, partners(size, step))
        step *= 2
    return value


def gathered(block, axis):
    size = lax.axis_size(axis)
    held = {0: block}
    step = size // 2
    while step:
        for k in sorted(held):
            held[k ^ step] = lax.ppermute(held[k], axis, partners(size, step))
        step //= 2
    return [held[k] for k in range(size)]


def attend_kernel(count, scale, chunk, *refs):
    handed_ref = refs[0]
    blocks = refs[1 : 1 + count]
    outs = refs[1 + count : 1 + 2 * count]
    q_s, k_s, v_s, g_s, dq_s, dk_s, dv_s = refs[1 + 2 * count :]
    rows = blocks[0].shape[1]
    length = rows * count
    seen = handed_ref.shape[0] // count
    for j, block in enumerate(blocks):
        at = pl.ds(j * rows, rows)
        q_s[at] = block[0]
        k_s[at] = block[1]
        v_s[at] = block[2]
    token = lax.broadcasted_iota(jnp.int32, (rows, seen), 0)
    source = lax.broadcasted_iota(jnp.int32, (rows, seen), 1)
    spread = jnp.where(
        (token // (2 * GW)) * (GW // 2) + (token % GW) // 2 == source, 1.0, 0.0
    ).astype(jnp.bfloat16)
    for j in range(count):
        g_s[pl.ds(j * rows, rows)] = jnp.dot(
            spread, handed_ref[pl.ds(j * seen, seen)], preferred_element_type=jnp.float32
        ).astype(jnp.bfloat16)
    dk_s[...] = jnp.zeros_like(dk_s)
    dv_s[...] = jnp.zeros_like(dv_s)
    key_rows = k_s[...]
    value_rows = v_s[...]
    key_columns = key_rows.T
    both_last = (((1,), (1,)), ((), ()))

    def step(c, carry):
        at = pl.ds(pl.multiple_of(c * chunk, chunk), chunk)
        q = q_s[at]
        g = g_s[at]
        scores = lax.dot_general(key_rows, q, both_last, preferred_element_type=jnp.float32) * scale
        exp_scores = jnp.exp(scores - jnp.max(scores, axis=0, keepdims=True))
        weights = exp_scores * (1.0 / jnp.sum(exp_scores, axis=0, keepdims=True))
        grad_weights = lax.dot_general(value_rows, g, both_last, preferred_element_type=jnp.float32)
        row_dot = jnp.sum(weights * grad_weights, axis=0, keepdims=True)
        grad_scores = (weights * (grad_weights - row_dot)).astype(jnp.bfloat16)
        dv_s[...] += jnp.dot(weights.astype(jnp.bfloat16), g, preferred_element_type=jnp.float32)
        dk_s[...] += jnp.dot(grad_scores, q, preferred_element_type=jnp.float32)
        dq = jnp.dot(key_columns, grad_scores, preferred_element_type=jnp.float32)
        dq_s[at] = (dq * scale).T.astype(jnp.bfloat16)
        return carry

    lax.fori_loop(0, length // chunk, step, 0)
    for j, out in enumerate(outs):
        at = pl.ds(j * rows, rows)
        out[0] = dq_s[at]
        out[1] = (dk_s[at] * scale).astype(jnp.bfloat16)
        out[2] = dv_s[at].astype(jnp.bfloat16)


def attend(handed, blocks, first, skip, heads):
    count = len(blocks)
    rows = blocks[0].shape[1]
    length = rows * count
    chunk = min(256, length)
    out_spec = pl.BlockSpec((3, rows, HD), lambda h: (0, 0, h))
    block_spec = pl.BlockSpec((3, rows, HD), lambda h: (0, 0, skip + h))
    return pl.pallas_call(
        functools.partial(attend_kernel, count, HD**-0.5, chunk),
        grid=(heads,),
        in_specs=[pl.BlockSpec((handed.shape[0], HD), lambda h: (0, first + h))]
        + [block_spec] * count,
        out_specs=[out_spec] * count,
        scratch_shapes=[pltpu.VMEM((length, HD), jnp.bfloat16)] * 5
        + [pltpu.VMEM((length, HD), jnp.float32)] * 2,
        out_shape=[jax.ShapeDtypeStruct((3, rows, heads * HD), jnp.bfloat16)] * count,
        cost_estimate=pl.CostEstimate(
            flops=10 * heads * length * length * HD,
            bytes_accessed=12 * length * heads * HD,
            transcendentals=heads * length * length,
        ),
        compiler_params=pltpu.CompilerParams(
            vmem_limit_bytes=(4 << 20) + 48 * length * chunk
        ),
    )(handed, *blocks)


def place_kernel(count, first, *refs):
    here = refs[0][0]
    parts = refs[1 : 1 + count]
    outs = refs[-4:-1]
    sems = refs[-1]
    width = parts[0].shape[2]
    own_width = outs[0].shape[2] // count
    copies = []
    for k, part in enumerate(parts):
        column = pl.multiple_of((here ^ k) * own_width + first, HD)
        for i, out in enumerate(outs):
            copies.append(
                pltpu.make_async_copy(
                    part.at[i], out.at[0, :, pl.ds(column, width)], sems.at[3 * k + i]
                )
            )
    for copy in copies:
        copy.start()
    for copy in copies:
        copy.wait()


def place(here, parts, outs, shape, first):
    count = len(parts)
    anywhere = pl.BlockSpec(memory_space=pl.ANY)
    held = len(outs)
    return pl.pallas_call(
        functools.partial(place_kernel, count, first),
        in_specs=[pl.BlockSpec(memory_space=pltpu.SMEM)]
        + [pl.BlockSpec(memory_space=pltpu.VMEM)] * count
        + [anywhere] * held,
        out_specs=[anywhere] * 3,
        out_shape=[jax.ShapeDtypeStruct(shape, jnp.bfloat16)] * 3,
        input_output_aliases={1 + count + i: i for i in range(held)},
        scratch_shapes=[pltpu.SemaphoreType.DMA((3 * count,))],
        cost_estimate=pl.CostEstimate(
            flops=0, bytes_accessed=4 * count * parts[0].size, transcendentals=0
        ),
        compiler_params=pltpu.CompilerParams(
            vmem_limit_bytes=(1 << 20) + 2 * count * parts[0].size
        ),
    )(here, *parts, *outs)


def work(
    rm_hidden, rm_cotangent, rm_gain, rewards, visual_pos, bridge, img_query, img_key, img_value
):
    count = lax.axis_size("tensor")
    here = lax.axis_index("tensor")
    place_of = here[None].astype(jnp.int32)
    own_width = img_query.shape[2] // count
    own = (img_query, img_key, img_value)
    visual_grad = visual_grads(place_of, visual_pos, rm_hidden, rm_cotangent, rm_gain)
    visual_blocks = gathered(visual_grad, "tensor")

    arrived = []
    for heads in split(own_width // HD, IN_HEADS):
        packed = pack(place_of, own, len(arrived) * HD, heads * HD, count)
        blocks = [packed[0]] + [
            lax.ppermute(packed[k], "tensor", partners(count, k)) for k in range(1, count)
        ]
        arrived += [(blocks, skip) for skip in range(heads)]

    reward_sum = total_over(jnp.sum(rewards), "dp")
    sample_count = lax.axis_size("dp") * rewards.shape[0]
    reward_weight = rewards[0] * sample_count / reward_sum
    handed = (
        jnp.dot(
            jnp.concatenate(visual_blocks, axis=0), bridge, preferred_element_type=jnp.float32
        )
        * reward_weight
    ).astype(jnp.bfloat16)

    outs = ()
    first = 0
    for heads in split(own_width // HD, OUT_HEADS):
        blocks, skip = arrived[first]
        grads = attend(handed, blocks, first, skip, heads)
        parts = [grads[0]] + [
            lax.ppermute(grads[k], "tensor", partners(count, k)) for k in range(1, count)
        ]
        outs = place(place_of, parts, outs, img_query.shape, first * HD)
        first += heads
    return tuple(outs)


def solution(mesh):
    placed = (
        P("dp", "tensor", None),
        P("dp", "tensor", None),
        P(),
        P("dp"),
        P("dp", "tensor"),
        P(None, "tensor"),
        P("dp", "tensor", None),
        P("dp", "tensor", None),
        P("dp", "tensor", None),
    )
    return jax.shard_map(
        work,
        mesh=mesh,
        in_specs=placed,
        out_specs=(P("dp", "tensor", None), P("dp", "tensor", None), P("dp", "tensor", None)),
        check_vma=False,
    )
```

```python
import functools

import jax
import jax.numpy as jnp
from jax import lax
from jax.experimental import pallas as pl
from jax.experimental.pallas import tpu as pltpu
from jax.sharding import PartitionSpec as P


HD = 128
GW = 64


def in_hbm(array):
    return pltpu.with_memory_space_constraint(array, pltpu.HBM)


def visual_kernel(
    here_ref, pos_hbm, gain_hbm, hidden_hbm, cot_hbm, out_ref, pos_ref, gain_ref, held, small, sems
):
    rows = hidden_hbm.shape[1]
    picked = out_ref.shape[0]
    pieces = sems.shape[1]
    piece = rows // pieces
    pos_copy = pltpu.make_async_copy(pos_hbm, pos_ref, small.at[0])
    copies = [pltpu.make_async_copy(gain_hbm, gain_ref, small.at[1])]
    pos_copy.start()
    for i, source in enumerate((hidden_hbm, cot_hbm)):
        for j in range(pieces):
            at = pl.ds(j * piece, piece)
            copies.append(
                pltpu.make_async_copy(source.at[0, at], held.at[i, at], sems.at[i, j])
            )
    for copy in copies:
        copy.start()
    pos_copy.wait()
    row = lax.broadcasted_iota(jnp.int32, (rows, picked), 0) + here_ref[0] * rows
    pick = jnp.where(row == pos_ref[...], 1.0, 0.0).astype(jnp.bfloat16)
    first_both = (((0,), (0,)), ((), ()))
    for copy in copies:
        copy.wait()
    hidden = lax.dot_general(pick, held[0], first_both, preferred_element_type=jnp.float32)
    cot = lax.dot_general(pick, held[1], first_both, preferred_element_type=jnp.float32)
    lanes = gain_ref.shape[1]
    scaled_cot = jnp.concatenate(
        [
            cot[:, j * lanes : (j + 1) * lanes] * gain_ref[pl.ds(j, 1)]
            for j in range(gain_ref.shape[0])
        ],
        axis=1,
    )
    inv_rms = lax.rsqrt(jnp.mean(hidden * hidden, axis=-1, keepdims=True) + 1e-06)
    mixed = jnp.mean(hidden * scaled_cot, axis=-1, keepdims=True)
    out_ref[...] = (inv_rms * scaled_cot - hidden * (inv_rms * inv_rms * inv_rms * mixed)).astype(
        jnp.bfloat16
    )


def visual_grads(here, positions, hidden, cotangent, gain):
    picked, depth = positions.shape[1], hidden.shape[2]
    rows = hidden.shape[1]
    pieces = 8 if rows % 64 == 0 else 1
    vmem = pl.BlockSpec(memory_space=pltpu.VMEM)
    hbm = pl.BlockSpec(memory_space=pltpu.HBM)
    return pl.pallas_call(
        visual_kernel,
        in_specs=[pl.BlockSpec(memory_space=pltpu.SMEM)] + [hbm] * 4,
        out_specs=vmem,
        scratch_shapes=[
            pltpu.VMEM(positions.shape, jnp.int32),
            pltpu.VMEM((depth // HD, HD), jnp.float32),
            pltpu.VMEM((2, rows, depth), jnp.bfloat16),
            pltpu.SemaphoreType.DMA((2,)),
            pltpu.SemaphoreType.DMA((2, pieces)),
        ],
        out_shape=jax.ShapeDtypeStruct((picked, depth), jnp.bfloat16),
        cost_estimate=pl.CostEstimate(
            flops=4 * picked * hidden.size, bytes_accessed=4 * hidden.size, transcendentals=0
        ),
        compiler_params=pltpu.CompilerParams(vmem_limit_bytes=(8 << 20) + 12 * hidden.size),
        name="visual",
    )(here, *map(in_hbm, (positions, gain.reshape(-1, HD), hidden, cotangent)))


def pack_kernel(count, first, slots, here_ref, *refs):
    sources, outs, sems = refs[:3], refs[3:-1], refs[-1]
    width = outs[0].shape[2] // len(slots)
    own_width = sources[0].shape[2] // count
    copies = []
    for k, out in enumerate(outs):
        for j, slot in enumerate(slots):
            column = pl.multiple_of((here_ref[0] ^ k ^ slot) * own_width + first, HD)
            for i in range(out.shape[0]):
                copies.append(
                    pltpu.make_async_copy(
                        sources[i].at[0, :, pl.ds(column, width)],
                        out.at[i, :, pl.ds(j * width, width)],
                        sems.at[len(copies)],
                    )
                )
    for copy in copies:
        copy.start()
    for copy in copies:
        copy.wait()


def pack(here, sources, first, width, slots, taken):
    count, rows = len(taken), sources[0].shape[1]
    total = sum(taken) * len(slots)
    return pl.pallas_call(
        functools.partial(pack_kernel, count, first, slots),
        in_specs=[pl.BlockSpec(memory_space=pltpu.SMEM)]
        + [pl.BlockSpec(memory_space=pltpu.HBM)] * 3,
        out_specs=[pl.BlockSpec(memory_space=pltpu.VMEM)] * count,
        out_shape=[
            jax.ShapeDtypeStruct((n, rows, width * len(slots)), jnp.bfloat16) for n in taken
        ],
        scratch_shapes=[pltpu.SemaphoreType.DMA((total,))],
        cost_estimate=pl.CostEstimate(
            flops=0, bytes_accessed=4 * total * rows * width, transcendentals=0
        ),
        compiler_params=pltpu.CompilerParams(
            vmem_limit_bytes=(1 << 20) + 2 * total * rows * width
        ),
    )(here, *map(in_hbm, sources))


def partners(size, k):
    return [(i, i ^ k) for i in range(size)]


def total_over(value, axis):
    size = lax.axis_size(axis)
    step = 1
    while step < size:
        value = value + lax.ppermute(value, axis, partners(size, step))
        step *= 2
    return value


def gathered(block, axis):
    size = lax.axis_size(axis)
    held = {0: block}
    step = size // 2
    while step:
        for k in sorted(held):
            held[k ^ step] = lax.ppermute(held[k], axis, partners(size, step))
        step //= 2
    return [held[k] for k in range(size)]


def spread_rows(rows, seen):
    token = lax.broadcasted_iota(jnp.int32, (rows, seen), 0)
    source = lax.broadcasted_iota(jnp.int32, (rows, seen), 1)
    return jnp.where(
        (token // (2 * GW)) * (GW // 2) + (token % GW) // 2 == source, 1.0, 0.0
    ).astype(jnp.bfloat16)


BOTH_LAST = (((1,), (1,)), ((), ()))


def attend_kernel(count, scale, chunk, *refs):
    handed_ref = refs[0]
    blocks = refs[1 : 1 + count]
    outs = refs[1 + count : 1 + 2 * count]
    q_s, k_s, v_s, g_s, dq_s, dk_s, dv_s = refs[1 + 2 * count :]
    rows = blocks[0].shape[1]
    length = rows * count
    seen = handed_ref.shape[0] // count
    for j, block in enumerate(blocks):
        at = pl.ds(j * rows, rows)
        q_s[at] = block[0]
        k_s[at] = block[1]
        v_s[at] = block[2]
    spread = spread_rows(rows, seen)
    for j in range(count):
        g_s[pl.ds(j * rows, rows)] = jnp.dot(
            spread, handed_ref[pl.ds(j * seen, seen)], preferred_element_type=jnp.float32
        ).astype(jnp.bfloat16)
    dk_s[...] = jnp.zeros_like(dk_s)
    dv_s[...] = jnp.zeros_like(dv_s)
    key_rows = k_s[...]
    value_rows = v_s[...]
    key_columns = key_rows.T

    def step(c, carry):
        at = pl.ds(pl.multiple_of(c * chunk, chunk), chunk)
        q = q_s[at]
        g = g_s[at]
        scores = lax.dot_general(key_rows, q, BOTH_LAST, preferred_element_type=jnp.float32) * scale
        exp_scores = jnp.exp(scores - jnp.max(scores, axis=0, keepdims=True))
        weights = exp_scores * (1.0 / jnp.sum(exp_scores, axis=0, keepdims=True))
        grad_weights = lax.dot_general(value_rows, g, BOTH_LAST, preferred_element_type=jnp.float32)
        row_dot = jnp.sum(weights * grad_weights, axis=0, keepdims=True)
        grad_scores = (weights * (grad_weights - row_dot)).astype(jnp.bfloat16)
        dv_s[...] += jnp.dot(weights.astype(jnp.bfloat16), g, preferred_element_type=jnp.float32)
        dk_s[...] += jnp.dot(grad_scores, q, preferred_element_type=jnp.float32)
        dq = jnp.dot(key_columns, grad_scores, preferred_element_type=jnp.float32)
        dq_s[at] = (dq * scale).T.astype(jnp.bfloat16)
        return carry

    lax.fori_loop(0, length // chunk, step, 0)
    for j, out in enumerate(outs):
        at = pl.ds(j * rows, rows)
        out[0] = dq_s[at]
        out[1] = (dk_s[at] * scale).astype(jnp.bfloat16)
        out[2] = dv_s[at].astype(jnp.bfloat16)


def attend(handed, blocks, first, skip, heads):
    count = len(blocks)
    rows = blocks[0].shape[1]
    length = rows * count
    chunk = min(256, length)
    out_spec = pl.BlockSpec((3, rows, HD), lambda h: (0, 0, h))
    block_spec = pl.BlockSpec((3, rows, HD), lambda h: (0, 0, skip + h))
    return pl.pallas_call(
        functools.partial(attend_kernel, count, HD**-0.5, chunk),
        grid=(heads,),
        in_specs=[pl.BlockSpec((handed.shape[0], HD), lambda h: (0, first + h))]
        + [block_spec] * count,
        out_specs=[out_spec] * count,
        scratch_shapes=[pltpu.VMEM((length, HD), jnp.bfloat16)] * 5
        + [pltpu.VMEM((length, HD), jnp.float32)] * 2,
        out_shape=[jax.ShapeDtypeStruct((3, rows, heads * HD), jnp.bfloat16)] * count,
        cost_estimate=pl.CostEstimate(
            flops=10 * heads * length * length * HD,
            bytes_accessed=12 * length * heads * HD,
            transcendentals=heads * length * length,
        ),
        compiler_params=pltpu.CompilerParams(
            vmem_limit_bytes=(4 << 20) + 48 * length * chunk
        ),
    )(handed, *blocks)


def load_half(count, handed_ref, far_handed_ref, blocks, q_s, k_s, v_s, g_s):
    half, rows = count // 2, blocks[0].shape[1]
    seen = handed_ref.shape[0] // count
    for j, block in enumerate(blocks):
        at = pl.ds(j * rows, rows)
        q_s[at] = block[0]
        if j < half:
            k_s[at] = block[1]
            v_s[at] = block[2]
    spread = spread_rows(rows, seen)

    def fill(ref, swap):
        for j in range(count):
            g_s[pl.ds(j * rows, rows)] = jnp.dot(
                spread, ref[pl.ds((j ^ swap) * seen, seen)], preferred_element_type=jnp.float32
            ).astype(jnp.bfloat16)

    own = pl.program_id(0) < pl.num_programs(0) // 2

    @pl.when(own)
    def _():
        fill(handed_ref, 0)

    @pl.when(jnp.logical_not(own))
    def _():
        fill(far_handed_ref, half)


def half_products(scale, key_rows, value_rows, q, g):
    scores = lax.dot_general(key_rows, q, BOTH_LAST, preferred_element_type=jnp.float32) * scale
    grad_weights = lax.dot_general(value_rows, g, BOTH_LAST, preferred_element_type=jnp.float32)
    return scores, grad_weights


def half_stats_kernel(count, scale, chunk, *refs):
    handed_ref, far_handed_ref = refs[:2]
    blocks = refs[2 : 2 + count]
    out, q_s, k_s, v_s, g_s = refs[2 + count :]
    load_half(count, handed_ref, far_handed_ref, blocks, q_s, k_s, v_s, g_s)
    key_rows, value_rows = k_s[...], v_s[...]

    def step(c, carry):
        at = pl.ds(pl.multiple_of(c * chunk, chunk), chunk)
        scores, grad_weights = half_products(scale, key_rows, value_rows, q_s[at], g_s[at])
        row_max = jnp.max(scores, axis=0, keepdims=True)
        exp_scores = jnp.exp(scores - row_max)
        total = jnp.sum(exp_scores, axis=0, keepdims=True)
        out[0, pl.ds(0, 1), at] = row_max + jnp.log(total)
        out[0, pl.ds(1, 1), at] = (
            jnp.sum(exp_scores * grad_weights, axis=0, keepdims=True) / total
        )
        return carry

    lax.fori_loop(0, q_s.shape[0] // chunk, step, 0)


def half_grads_kernel(count, scale, chunk, *refs):
    handed_ref, far_handed_ref = refs[:2]
    blocks = refs[2 : 2 + count]
    stats_ref, far_stats_ref = refs[2 + count : 4 + count]
    outs = refs[4 + count : 4 + 2 * count]
    q_s, k_s, v_s, g_s, dq_s, dk_s, dv_s = refs[4 + 2 * count :]
    load_half(count, handed_ref, far_handed_ref, blocks, q_s, k_s, v_s, g_s)
    rows, length = blocks[0].shape[1], q_s.shape[0]
    dk_s[...] = jnp.zeros_like(dk_s)
    dv_s[...] = jnp.zeros_like(dv_s)
    key_rows, value_rows = k_s[...], v_s[...]
    key_columns = key_rows.T

    def step(c, carry):
        at = pl.ds(pl.multiple_of(c * chunk, chunk), chunk)
        far_first = lax.rem(c * chunk + length // 2, length)
        far_at = pl.ds(pl.multiple_of(far_first, chunk), chunk)
        q, g = q_s[at], g_s[at]
        scores, grad_weights = half_products(scale, key_rows, value_rows, q, g)
        near, far = stats_ref[0, pl.ds(0, 1), at], far_stats_ref[0, pl.ds(0, 1), far_at]
        top = jnp.maximum(near, far)
        whole = top + jnp.log(jnp.exp(near - top) + jnp.exp(far - top))
        row_dot = (
            jnp.exp(near - whole) * stats_ref[0, pl.ds(1, 1), at]
            + jnp.exp(far - whole) * far_stats_ref[0, pl.ds(1, 1), far_at]
        )
        weights = jnp.exp(scores - whole)
        grad_scores = (weights * (grad_weights - row_dot)).astype(jnp.bfloat16)
        dv_s[...] += jnp.dot(weights.astype(jnp.bfloat16), g, preferred_element_type=jnp.float32)
        dk_s[...] += jnp.dot(grad_scores, q, preferred_element_type=jnp.float32)
        dq = jnp.dot(key_columns, grad_scores, preferred_element_type=jnp.float32)
        dq_s[at] = (dq * scale).T.astype(jnp.bfloat16)
        return carry

    lax.fori_loop(0, length // chunk, step, 0)
    for j, out in enumerate(outs):
        at = pl.ds(j * rows, rows)
        out[0] = dq_s[at]
        if j < count // 2:
            out[1] = (dk_s[at] * scale).astype(jnp.bfloat16)
            out[2] = dv_s[at].astype(jnp.bfloat16)


def half_call(kernel, handed, far_handed, blocks, stats, first):
    count = len(blocks)
    rows, heads = blocks[0].shape[1], blocks[0].shape[2] // HD
    length, held = rows * count, rows * count // 2
    chunk = min(256, held)
    each = heads // 2

    def block_spec(array):
        return pl.BlockSpec((array.shape[0], rows, HD), lambda h: (0, 0, h))

    stats_spec = pl.BlockSpec((1, 2, length), lambda h: (h, 0, 0))
    far_spec = pl.BlockSpec((1, 2, length), lambda h: (lax.rem(h + each, heads), 0, 0))
    scratch = [pltpu.VMEM((n, HD), jnp.bfloat16) for n in (length, held, held, length)]
    if stats:
        out_specs = [block_spec(b) for b in blocks]
        out_shape = [jax.ShapeDtypeStruct(b.shape, jnp.bfloat16) for b in blocks]
        scratch += [pltpu.VMEM((length, HD), jnp.bfloat16)]
        scratch += [pltpu.VMEM((held, HD), jnp.float32)] * 2
    else:
        out_specs = stats_spec
        out_shape = jax.ShapeDtypeStruct((heads, 2, length), jnp.float32)
    return pl.pallas_call(
        functools.partial(kernel, count, HD**-0.5, chunk),
        grid=(heads,),
        in_specs=[
            pl.BlockSpec((handed.shape[0], HD), lambda h: (0, first + lax.rem(h, each))),
            pl.BlockSpec((handed.shape[0], HD), lambda h: (0, lax.rem(h, each))),
        ]
        + [block_spec(b) for b in blocks]
        + [stats_spec, far_spec][: len(stats)],
        out_specs=out_specs,
        scratch_shapes=scratch,
        out_shape=out_shape,
        cost_estimate=pl.CostEstimate(
            flops=(10 if stats else 4) * heads * length * held * HD,
            bytes_accessed=12 * length * heads * HD,
            transcendentals=heads * length * held,
        ),
        compiler_params=pltpu.CompilerParams(
            vmem_limit_bytes=(4 << 20) + 48 * length * chunk
        ),
    )(handed, far_handed, *blocks, *stats)


def place_kernel(count, first, *refs):
    here = refs[0][0]
    parts = refs[1 : 1 + count]
    outs = refs[-4:-1]
    sems = refs[-1]
    width = parts[0].shape[2]
    own_width = outs[0].shape[2] // count
    copies = []
    for k, part in enumerate(parts):
        column = pl.multiple_of((here ^ k) * own_width + first, HD)
        for i, out in enumerate(outs):
            copies.append(
                pltpu.make_async_copy(
                    part.at[i], out.at[0, :, pl.ds(column, width)], sems.at[3 * k + i]
                )
            )
    for copy in copies:
        copy.start()
    for copy in copies:
        copy.wait()


def place(here, parts, outs, shape, first):
    count = len(parts)
    anywhere = pl.BlockSpec(memory_space=pl.ANY)
    held = len(outs)
    return pl.pallas_call(
        functools.partial(place_kernel, count, first),
        in_specs=[pl.BlockSpec(memory_space=pltpu.SMEM)]
        + [pl.BlockSpec(memory_space=pltpu.VMEM)] * count
        + [anywhere] * held,
        out_specs=[anywhere] * 3,
        out_shape=[jax.ShapeDtypeStruct(shape, jnp.bfloat16)] * 3,
        input_output_aliases={1 + count + i: i for i in range(held)},
        scratch_shapes=[pltpu.SemaphoreType.DMA((3 * count,))],
        cost_estimate=pl.CostEstimate(
            flops=0, bytes_accessed=4 * count * parts[0].size, transcendentals=0
        ),
        compiler_params=pltpu.CompilerParams(
            vmem_limit_bytes=(1 << 20) + 2 * count * parts[0].size
        ),
    )(here, *parts, *outs)


def place_half_kernel(count, first, *refs):
    here = refs[0][0]
    parts = refs[1 : 1 + count]
    outs = refs[4 + count : 7 + count]
    added, sems = refs[7 + count :]
    half, width = count // 2, parts[0].shape[2] // 2
    own_width = outs[0].shape[2] // count
    copies = []

    def put(source, out, shard):
        column = pl.multiple_of((here ^ shard) * own_width + first, HD)
        copy = pltpu.make_async_copy(
            source, out.at[0, :, pl.ds(column, width)], sems.at[len(copies)]
        )
        copy.start()
        copies.append(copy)

    for k in range(half):
        for slot in range(2):
            for i in (1, 2):
                put(parts[k].at[i, :, pl.ds(slot * width, width)], outs[i], k ^ (half * slot))
    for shard in range(count):
        near = parts[shard][0, :, pl.ds(0, width)].astype(jnp.float32)
        far = parts[shard ^ half][0, :, pl.ds(width, width)].astype(jnp.float32)
        added[shard] = (near + far).astype(jnp.bfloat16)
        put(added.at[shard], outs[0], shard)
    for copy in copies:
        copy.wait()


def place_half(here, parts, outs, first):
    count, (rows, width) = len(parts), parts[0].shape[1:]
    anywhere = pl.BlockSpec(memory_space=pl.ANY)
    return pl.pallas_call(
        functools.partial(place_half_kernel, count, first),
        in_specs=[pl.BlockSpec(memory_space=pltpu.SMEM)]
        + [pl.BlockSpec(memory_space=pltpu.VMEM)] * count
        + [anywhere] * 3,
        out_specs=[anywhere] * 3,
        out_shape=[jax.ShapeDtypeStruct(out.shape, out.dtype) for out in outs],
        input_output_aliases={1 + count + i: i for i in range(3)},
        scratch_shapes=[
            pltpu.VMEM((count, rows, width // 2), jnp.bfloat16),
            pltpu.SemaphoreType.DMA((3 * count,)),
        ],
        cost_estimate=pl.CostEstimate(
            flops=0, bytes_accessed=4 * count * parts[0].size, transcendentals=0
        ),
        compiler_params=pltpu.CompilerParams(
            vmem_limit_bytes=(1 << 20) + 4 * count * parts[0].size
        ),
        name="place_half",
    )(here, *parts, *outs)


def work(
    rm_hidden, rm_cotangent, rm_gain, rewards, visual_pos, bridge, img_query, img_key, img_value
):
    count = lax.axis_size("tensor")
    here = lax.axis_index("tensor")
    place_of = here[None].astype(jnp.int32)
    own_width = img_query.shape[2] // count
    heads = own_width // HD
    shared = heads // 2
    whole = heads - shared
    half = count // 2
    own = (img_query, img_key, img_value)

    def exchange(blocks):
        return [blocks[0]] + [
            lax.ppermute(blocks[k], "tensor", partners(count, k)) for k in range(1, count)
        ]

    visual_grad = visual_grads(place_of, visual_pos, rm_hidden, rm_cotangent, rm_gain)
    visual_blocks = gathered(visual_grad, "tensor")
    blocks = exchange(pack(place_of, own, 0, whole * HD, (0,), (3,) * count))
    if shared:
        taken = (3,) * half + (1,) * half
        packed = pack(place_of, own, whole * HD, shared * HD, (0, half), taken)
        half_blocks = exchange(packed)

    reward_sum = total_over(jnp.sum(rewards), "dp")
    sample_count = lax.axis_size("dp") * rewards.shape[0]
    reward_weight = rewards[0] * sample_count / reward_sum
    handed = (
        jnp.dot(
            jnp.concatenate(visual_blocks, axis=0), bridge, preferred_element_type=jnp.float32
        )
        * reward_weight
    ).astype(jnp.bfloat16)
    if shared:
        far_handed = lax.ppermute(handed[:, whole * HD :], "tensor", partners(count, half))

    outs = ()
    for g in range(whole):
        parts = exchange(attend(handed, blocks, g, g, 1))
        outs = place(place_of, parts, outs, img_query.shape, g * HD)
    if shared:
        stats = half_call(half_stats_kernel, handed, far_handed, half_blocks, (), whole)
        far_stats = lax.ppermute(stats, "tensor", partners(count, half))
        grads = half_call(
            half_grads_kernel, handed, far_handed, half_blocks, (stats, far_stats), whole
        )
        outs = place_half(place_of, exchange(grads), outs, whole * HD)
    return tuple(outs)


def solution(mesh):
    placed = (
        P("dp", "tensor", None),
        P("dp", "tensor", None),
        P(),
        P("dp"),
        P("dp", "tensor"),
        P(None, "tensor"),
        P("dp", "tensor", None),
        P("dp", "tensor", None),
        P("dp", "tensor", None),
    )
    return jax.shard_map(
        work,
        mesh=mesh,
        in_specs=placed,
        out_specs=(P("dp", "tensor", None), P("dp", "tensor", None), P("dp", "tensor", None)),
        check_vma=False,
    )
```

```python
import functools

import jax
import jax.numpy as jnp
from jax import lax
from jax.experimental import pallas as pl
from jax.experimental.pallas import tpu as pltpu
from jax.sharding import PartitionSpec as P


HD = 128
GW = 64


def in_hbm(array):
    return pltpu.with_memory_space_constraint(array, pltpu.HBM)


def visual_kernel(
    here_ref, pos_hbm, gain_hbm, hidden_hbm, cot_hbm, out_ref, pos_ref, gain_ref, held, small, sems
):
    rows = hidden_hbm.shape[1]
    picked = out_ref.shape[0]
    pieces = sems.shape[1]
    piece = rows // pieces
    pos_copy = pltpu.make_async_copy(pos_hbm, pos_ref, small.at[0])
    copies = [pltpu.make_async_copy(gain_hbm, gain_ref, small.at[1])]
    pos_copy.start()
    for i, source in enumerate((hidden_hbm, cot_hbm)):
        for j in range(pieces):
            at = pl.ds(j * piece, piece)
            copies.append(
                pltpu.make_async_copy(source.at[0, at], held.at[i, at], sems.at[i, j])
            )
    for copy in copies:
        copy.start()
    pos_copy.wait()
    row = lax.broadcasted_iota(jnp.int32, (rows, picked), 0) + here_ref[0] * rows
    pick = jnp.where(row == pos_ref[...], 1.0, 0.0).astype(jnp.bfloat16)
    first_both = (((0,), (0,)), ((), ()))
    for copy in copies:
        copy.wait()
    hidden = lax.dot_general(pick, held[0], first_both, preferred_element_type=jnp.float32)
    cot = lax.dot_general(pick, held[1], first_both, preferred_element_type=jnp.float32)
    lanes = gain_ref.shape[1]
    scaled_cot = jnp.concatenate(
        [
            cot[:, j * lanes : (j + 1) * lanes] * gain_ref[pl.ds(j, 1)]
            for j in range(gain_ref.shape[0])
        ],
        axis=1,
    )
    inv_rms = lax.rsqrt(jnp.mean(hidden * hidden, axis=-1, keepdims=True) + 1e-06)
    mixed = jnp.mean(hidden * scaled_cot, axis=-1, keepdims=True)
    out_ref[...] = (inv_rms * scaled_cot - hidden * (inv_rms * inv_rms * inv_rms * mixed)).astype(
        jnp.bfloat16
    )


def visual_grads(here, positions, hidden, cotangent, gain):
    picked, depth = positions.shape[1], hidden.shape[2]
    rows = hidden.shape[1]
    pieces = 8 if rows % 64 == 0 else 1
    vmem = pl.BlockSpec(memory_space=pltpu.VMEM)
    hbm = pl.BlockSpec(memory_space=pltpu.HBM)
    return pl.pallas_call(
        visual_kernel,
        in_specs=[pl.BlockSpec(memory_space=pltpu.SMEM)] + [hbm] * 4,
        out_specs=vmem,
        scratch_shapes=[
            pltpu.VMEM(positions.shape, jnp.int32),
            pltpu.VMEM((depth // HD, HD), jnp.float32),
            pltpu.VMEM((2, rows, depth), jnp.bfloat16),
            pltpu.SemaphoreType.DMA((2,)),
            pltpu.SemaphoreType.DMA((2, pieces)),
        ],
        out_shape=jax.ShapeDtypeStruct((picked, depth), jnp.bfloat16),
        cost_estimate=pl.CostEstimate(
            flops=4 * picked * hidden.size, bytes_accessed=4 * hidden.size, transcendentals=0
        ),
        compiler_params=pltpu.CompilerParams(vmem_limit_bytes=(8 << 20) + 12 * hidden.size),
        name="visual",
    )(here, *map(in_hbm, (positions, gain.reshape(-1, HD), hidden, cotangent)))


def pack_kernel(count, first, slots, here_ref, *refs):
    sources, outs, sems = refs[:3], refs[3:-1], refs[-1]
    width = outs[0].shape[2] // len(slots)
    own_width = sources[0].shape[2] // count
    copies = []
    for k, out in enumerate(outs):
        for j, slot in enumerate(slots):
            column = pl.multiple_of((here_ref[0] ^ k ^ slot) * own_width + first, HD)
            for i in range(out.shape[0]):
                copies.append(
                    pltpu.make_async_copy(
                        sources[i].at[0, :, pl.ds(column, width)],
                        out.at[i, :, pl.ds(j * width, width)],
                        sems.at[len(copies)],
                    )
                )
    for copy in copies:
        copy.start()
    for copy in copies:
        copy.wait()


def pack(here, sources, first, width, slots, taken):
    count, rows = len(taken), sources[0].shape[1]
    total = sum(taken) * len(slots)
    return pl.pallas_call(
        functools.partial(pack_kernel, count, first, slots),
        in_specs=[pl.BlockSpec(memory_space=pltpu.SMEM)]
        + [pl.BlockSpec(memory_space=pltpu.HBM)] * 3,
        out_specs=[pl.BlockSpec(memory_space=pltpu.VMEM)] * count,
        out_shape=[
            jax.ShapeDtypeStruct((n, rows, width * len(slots)), jnp.bfloat16) for n in taken
        ],
        scratch_shapes=[pltpu.SemaphoreType.DMA((total,))],
        cost_estimate=pl.CostEstimate(
            flops=0, bytes_accessed=4 * total * rows * width, transcendentals=0
        ),
        compiler_params=pltpu.CompilerParams(
            vmem_limit_bytes=(1 << 20) + 2 * total * rows * width
        ),
    )(here, *map(in_hbm, sources))


def partners(size, k):
    return [(i, i ^ k) for i in range(size)]


def total_over(value, axis):
    size = lax.axis_size(axis)
    step = 1
    while step < size:
        value = value + lax.ppermute(value, axis, partners(size, step))
        step *= 2
    return value


def gathered(block, axis):
    size = lax.axis_size(axis)
    held = {0: block}
    step = size // 2
    while step:
        for k in sorted(held):
            held[k ^ step] = lax.ppermute(held[k], axis, partners(size, step))
        step //= 2
    return [held[k] for k in range(size)]


def spread_rows(rows, seen):
    token = lax.broadcasted_iota(jnp.int32, (rows, seen), 0)
    source = lax.broadcasted_iota(jnp.int32, (rows, seen), 1)
    return jnp.where(
        (token // (2 * GW)) * (GW // 2) + (token % GW) // 2 == source, 1.0, 0.0
    ).astype(jnp.bfloat16)


BOTH_LAST = (((1,), (1,)), ((), ()))


def attend_kernel(count, scale, chunk, *refs):
    handed_ref = refs[0]
    blocks = refs[1 : 1 + count]
    outs = refs[1 + count : 1 + 2 * count]
    q_s, k_s, v_s, g_s, dq_s, dk_s, dv_s = refs[1 + 2 * count :]
    rows = blocks[0].shape[1]
    length = rows * count
    seen = handed_ref.shape[0] // count
    for j, block in enumerate(blocks):
        at = pl.ds(j * rows, rows)
        q_s[at] = block[0]
        k_s[at] = block[1]
        v_s[at] = block[2]
    spread = spread_rows(rows, seen)
    for j in range(count):
        g_s[pl.ds(j * rows, rows)] = jnp.dot(
            spread, handed_ref[pl.ds(j * seen, seen)], preferred_element_type=jnp.float32
        ).astype(jnp.bfloat16)
    dk_s[...] = jnp.zeros_like(dk_s)
    dv_s[...] = jnp.zeros_like(dv_s)
    key_rows = k_s[...]
    value_rows = v_s[...]
    key_columns = key_rows.T

    def step(c, carry):
        at = pl.ds(pl.multiple_of(c * chunk, chunk), chunk)
        q = q_s[at]
        g = g_s[at]
        scores = lax.dot_general(key_rows, q, BOTH_LAST, preferred_element_type=jnp.float32) * scale
        exp_scores = jnp.exp(scores - jnp.max(scores, axis=0, keepdims=True))
        weights = exp_scores * (1.0 / jnp.sum(exp_scores, axis=0, keepdims=True))
        grad_weights = lax.dot_general(value_rows, g, BOTH_LAST, preferred_element_type=jnp.float32)
        row_dot = jnp.sum(weights * grad_weights, axis=0, keepdims=True)
        grad_scores = (weights * (grad_weights - row_dot)).astype(jnp.bfloat16)
        dv_s[...] += jnp.dot(weights.astype(jnp.bfloat16), g, preferred_element_type=jnp.float32)
        dk_s[...] += jnp.dot(grad_scores, q, preferred_element_type=jnp.float32)
        dq = jnp.dot(key_columns, grad_scores, preferred_element_type=jnp.float32)
        dq_s[at] = (dq * scale).T.astype(jnp.bfloat16)
        return carry

    lax.fori_loop(0, length // chunk, step, 0, unroll=length <= 2 * chunk)
    for j, out in enumerate(outs):
        at = pl.ds(j * rows, rows)
        out[0] = dq_s[at]
        out[1] = (dk_s[at] * scale).astype(jnp.bfloat16)
        out[2] = dv_s[at].astype(jnp.bfloat16)


def attend(handed, blocks, first, skip, heads):
    count = len(blocks)
    rows = blocks[0].shape[1]
    length = rows * count
    chunk = min(256, length)
    out_spec = pl.BlockSpec((3, rows, HD), lambda h: (0, 0, h))
    block_spec = pl.BlockSpec((3, rows, HD), lambda h: (0, 0, skip + h))
    return pl.pallas_call(
        functools.partial(attend_kernel, count, HD**-0.5, chunk),
        grid=(heads,),
        in_specs=[pl.BlockSpec((handed.shape[0], HD), lambda h: (0, first + h))]
        + [block_spec] * count,
        out_specs=[out_spec] * count,
        scratch_shapes=[pltpu.VMEM((length, HD), jnp.bfloat16)] * 5
        + [pltpu.VMEM((length, HD), jnp.float32)] * 2,
        out_shape=[jax.ShapeDtypeStruct((3, rows, heads * HD), jnp.bfloat16)] * count,
        cost_estimate=pl.CostEstimate(
            flops=10 * heads * length * length * HD,
            bytes_accessed=12 * length * heads * HD,
            transcendentals=heads * length * length,
        ),
        compiler_params=pltpu.CompilerParams(
            vmem_limit_bytes=(4 << 20) + 48 * length * chunk
        ),
    )(handed, *blocks)


def load_half(count, handed_ref, far_handed_ref, blocks, q_s, k_s, v_s, g_s):
    half, rows = count // 2, blocks[0].shape[1]
    seen = handed_ref.shape[0] // count
    for j, block in enumerate(blocks):
        at = pl.ds(j * rows, rows)
        q_s[at] = block[0]
        if j < half:
            k_s[at] = block[1]
            v_s[at] = block[2]
    spread = spread_rows(rows, seen)

    def fill(ref, swap):
        for j in range(count):
            g_s[pl.ds(j * rows, rows)] = jnp.dot(
                spread, ref[pl.ds((j ^ swap) * seen, seen)], preferred_element_type=jnp.float32
            ).astype(jnp.bfloat16)

    own = pl.program_id(0) < pl.num_programs(0) // 2

    @pl.when(own)
    def _():
        fill(handed_ref, 0)

    @pl.when(jnp.logical_not(own))
    def _():
        fill(far_handed_ref, half)


def half_products(scale, key_rows, value_rows, q, g):
    scores = lax.dot_general(key_rows, q, BOTH_LAST, preferred_element_type=jnp.float32) * scale
    grad_weights = lax.dot_general(value_rows, g, BOTH_LAST, preferred_element_type=jnp.float32)
    return scores, grad_weights


def half_stats_kernel(count, scale, chunk, *refs):
    handed_ref, far_handed_ref = refs[:2]
    blocks = refs[2 : 2 + count]
    out, q_s, k_s, v_s, g_s = refs[2 + count :]
    load_half(count, handed_ref, far_handed_ref, blocks, q_s, k_s, v_s, g_s)
    key_rows, value_rows = k_s[...], v_s[...]

    def step(c, carry):
        at = pl.ds(pl.multiple_of(c * chunk, chunk), chunk)
        scores, grad_weights = half_products(scale, key_rows, value_rows, q_s[at], g_s[at])
        row_max = jnp.max(scores, axis=0, keepdims=True)
        exp_scores = jnp.exp(scores - row_max)
        total = jnp.sum(exp_scores, axis=0, keepdims=True)
        out[0, pl.ds(0, 1), at] = row_max + jnp.log(total)
        out[0, pl.ds(1, 1), at] = (
            jnp.sum(exp_scores * grad_weights, axis=0, keepdims=True) / total
        )
        return carry

    lax.fori_loop(0, q_s.shape[0] // chunk, step, 0, unroll=q_s.shape[0] <= 2 * chunk)


def half_grads_kernel(count, scale, chunk, *refs):
    handed_ref, far_handed_ref = refs[:2]
    blocks = refs[2 : 2 + count]
    stats_ref, far_stats_ref = refs[2 + count : 4 + count]
    outs = refs[4 + count : 4 + 2 * count]
    q_s, k_s, v_s, g_s, dq_s, dk_s, dv_s = refs[4 + 2 * count :]
    load_half(count, handed_ref, far_handed_ref, blocks, q_s, k_s, v_s, g_s)
    rows, length = blocks[0].shape[1], q_s.shape[0]
    dk_s[...] = jnp.zeros_like(dk_s)
    dv_s[...] = jnp.zeros_like(dv_s)
    key_rows, value_rows = k_s[...], v_s[...]
    key_columns = key_rows.T

    def step(c, carry):
        at = pl.ds(pl.multiple_of(c * chunk, chunk), chunk)
        far_first = lax.rem(c * chunk + length // 2, length)
        far_at = pl.ds(pl.multiple_of(far_first, chunk), chunk)
        q, g = q_s[at], g_s[at]
        scores, grad_weights = half_products(scale, key_rows, value_rows, q, g)
        near, far = stats_ref[0, pl.ds(0, 1), at], far_stats_ref[0, pl.ds(0, 1), far_at]
        top = jnp.maximum(near, far)
        whole = top + jnp.log(jnp.exp(near - top) + jnp.exp(far - top))
        row_dot = (
            jnp.exp(near - whole) * stats_ref[0, pl.ds(1, 1), at]
            + jnp.exp(far - whole) * far_stats_ref[0, pl.ds(1, 1), far_at]
        )
        weights = jnp.exp(scores - whole)
        grad_scores = (weights * (grad_weights - row_dot)).astype(jnp.bfloat16)
        dv_s[...] += jnp.dot(weights.astype(jnp.bfloat16), g, preferred_element_type=jnp.float32)
        dk_s[...] += jnp.dot(grad_scores, q, preferred_element_type=jnp.float32)
        dq = jnp.dot(key_columns, grad_scores, preferred_element_type=jnp.float32)
        dq_s[at] = (dq * scale).T.astype(jnp.bfloat16)
        return carry

    lax.fori_loop(0, length // chunk, step, 0, unroll=length <= 2 * chunk)
    for j, out in enumerate(outs):
        at = pl.ds(j * rows, rows)
        out[0] = dq_s[at]
        if j < count // 2:
            out[1] = (dk_s[at] * scale).astype(jnp.bfloat16)
            out[2] = dv_s[at].astype(jnp.bfloat16)


def half_call(kernel, handed, far_handed, blocks, stats, first):
    count = len(blocks)
    rows, heads = blocks[0].shape[1], blocks[0].shape[2] // HD
    length, held = rows * count, rows * count // 2
    chunk = min(256, held)
    each = heads // 2

    def block_spec(array):
        return pl.BlockSpec((array.shape[0], rows, HD), lambda h: (0, 0, h))

    stats_spec = pl.BlockSpec((1, 2, length), lambda h: (h, 0, 0))
    far_spec = pl.BlockSpec((1, 2, length), lambda h: (lax.rem(h + each, heads), 0, 0))
    scratch = [pltpu.VMEM((n, HD), jnp.bfloat16) for n in (length, held, held, length)]
    if stats:
        out_specs = [block_spec(b) for b in blocks]
        out_shape = [jax.ShapeDtypeStruct(b.shape, jnp.bfloat16) for b in blocks]
        scratch += [pltpu.VMEM((length, HD), jnp.bfloat16)]
        scratch += [pltpu.VMEM((held, HD), jnp.float32)] * 2
    else:
        out_specs = stats_spec
        out_shape = jax.ShapeDtypeStruct((heads, 2, length), jnp.float32)
    return pl.pallas_call(
        functools.partial(kernel, count, HD**-0.5, chunk),
        grid=(heads,),
        in_specs=[
            pl.BlockSpec((handed.shape[0], HD), lambda h: (0, first + lax.rem(h, each))),
            pl.BlockSpec((handed.shape[0], HD), lambda h: (0, lax.rem(h, each))),
        ]
        + [block_spec(b) for b in blocks]
        + [stats_spec, far_spec][: len(stats)],
        out_specs=out_specs,
        scratch_shapes=scratch,
        out_shape=out_shape,
        cost_estimate=pl.CostEstimate(
            flops=(10 if stats else 4) * heads * length * held * HD,
            bytes_accessed=12 * length * heads * HD,
            transcendentals=heads * length * held,
        ),
        compiler_params=pltpu.CompilerParams(
            vmem_limit_bytes=(4 << 20) + 48 * length * chunk
        ),
    )(handed, far_handed, *blocks, *stats)


def place_kernel(count, first, *refs):
    here = refs[0][0]
    parts = refs[1 : 1 + count]
    outs = refs[-4:-1]
    sems = refs[-1]
    width = parts[0].shape[2]
    own_width = outs[0].shape[2] // count
    copies = []
    for k, part in enumerate(parts):
        column = pl.multiple_of((here ^ k) * own_width + first, HD)
        for i, out in enumerate(outs):
            copies.append(
                pltpu.make_async_copy(
                    part.at[i], out.at[0, :, pl.ds(column, width)], sems.at[3 * k + i]
                )
            )
    for copy in copies:
        copy.start()
    for copy in copies:
        copy.wait()


def place(here, parts, outs, shape, first):
    count = len(parts)
    anywhere = pl.BlockSpec(memory_space=pl.ANY)
    held = len(outs)
    return pl.pallas_call(
        functools.partial(place_kernel, count, first),
        in_specs=[pl.BlockSpec(memory_space=pltpu.SMEM)]
        + [pl.BlockSpec(memory_space=pltpu.VMEM)] * count
        + [anywhere] * held,
        out_specs=[anywhere] * 3,
        out_shape=[jax.ShapeDtypeStruct(shape, jnp.bfloat16)] * 3,
        input_output_aliases={1 + count + i: i for i in range(held)},
        scratch_shapes=[pltpu.SemaphoreType.DMA((3 * count,))],
        cost_estimate=pl.CostEstimate(
            flops=0, bytes_accessed=4 * count * parts[0].size, transcendentals=0
        ),
        compiler_params=pltpu.CompilerParams(
            vmem_limit_bytes=(1 << 20) + 2 * count * parts[0].size
        ),
    )(here, *parts, *outs)


def place_half_kernel(count, first, *refs):
    here = refs[0][0]
    parts = refs[1 : 1 + count]
    outs = refs[4 + count : 7 + count]
    added, sems = refs[7 + count :]
    half, width = count // 2, parts[0].shape[2] // 2
    own_width = outs[0].shape[2] // count
    copies = []

    def put(source, out, shard):
        column = pl.multiple_of((here ^ shard) * own_width + first, HD)
        copy = pltpu.make_async_copy(
            source, out.at[0, :, pl.ds(column, width)], sems.at[len(copies)]
        )
        copy.start()
        copies.append(copy)

    for k in range(half):
        for slot in range(2):
            for i in (1, 2):
                put(parts[k].at[i, :, pl.ds(slot * width, width)], outs[i], k ^ (half * slot))
    for shard in range(count):
        near = parts[shard][0, :, pl.ds(0, width)].astype(jnp.float32)
        far = parts[shard ^ half][0, :, pl.ds(width, width)].astype(jnp.float32)
        added[shard] = (near + far).astype(jnp.bfloat16)
        put(added.at[shard], outs[0], shard)
    for copy in copies:
        copy.wait()


def place_half(here, parts, outs, first):
    count, (rows, width) = len(parts), parts[0].shape[1:]
    anywhere = pl.BlockSpec(memory_space=pl.ANY)
    return pl.pallas_call(
        functools.partial(place_half_kernel, count, first),
        in_specs=[pl.BlockSpec(memory_space=pltpu.SMEM)]
        + [pl.BlockSpec(memory_space=pltpu.VMEM)] * count
        + [anywhere] * 3,
        out_specs=[anywhere] * 3,
        out_shape=[jax.ShapeDtypeStruct(out.shape, out.dtype) for out in outs],
        input_output_aliases={1 + count + i: i for i in range(3)},
        scratch_shapes=[
            pltpu.VMEM((count, rows, width // 2), jnp.bfloat16),
            pltpu.SemaphoreType.DMA((3 * count,)),
        ],
        cost_estimate=pl.CostEstimate(
            flops=0, bytes_accessed=4 * count * parts[0].size, transcendentals=0
        ),
        compiler_params=pltpu.CompilerParams(
            vmem_limit_bytes=(1 << 20) + 4 * count * parts[0].size
        ),
        name="place_half",
    )(here, *parts, *outs)


def work(
    rm_hidden, rm_cotangent, rm_gain, rewards, visual_pos, bridge, img_query, img_key, img_value
):
    count = lax.axis_size("tensor")
    here = lax.axis_index("tensor")
    place_of = here[None].astype(jnp.int32)
    own_width = img_query.shape[2] // count
    heads = own_width // HD
    shared = heads // 2
    whole = heads - shared
    half = count // 2
    own = (img_query, img_key, img_value)

    def exchange(blocks):
        return [blocks[0]] + [
            lax.ppermute(blocks[k], "tensor", partners(count, k)) for k in range(1, count)
        ]

    visual_grad = visual_grads(place_of, visual_pos, rm_hidden, rm_cotangent, rm_gain)
    visual_blocks = gathered(visual_grad, "tensor")
    if shared:
        taken = (3,) * half + (1,) * half
        packed = pack(place_of, own, whole * HD, shared * HD, (0, half), taken)
        half_blocks = exchange(packed)
    whole_blocks = [
        exchange(pack(place_of, own, g * HD, HD, (0,), (3,) * count))
        for g in range(whole)
    ]

    reward_sum = total_over(jnp.sum(rewards), "dp")
    sample_count = lax.axis_size("dp") * rewards.shape[0]
    reward_weight = rewards[0] * sample_count / reward_sum
    handed = (
        jnp.dot(
            jnp.concatenate(visual_blocks, axis=0), bridge, preferred_element_type=jnp.float32
        )
        * reward_weight
    ).astype(jnp.bfloat16)
    if shared:
        far_handed = lax.ppermute(handed[:, whole * HD :], "tensor", partners(count, half))

    outs = ()
    for g in range(whole):
        parts = exchange(attend(handed, whole_blocks[g], g, 0, 1))
        outs = place(place_of, parts, outs, img_query.shape, g * HD)
    if shared:
        stats = half_call(half_stats_kernel, handed, far_handed, half_blocks, (), whole)
        far_stats = lax.ppermute(stats, "tensor", partners(count, half))
        grads = half_call(
            half_grads_kernel, handed, far_handed, half_blocks, (stats, far_stats), whole
        )
        outs = place_half(place_of, exchange(grads), outs, whole * HD)
    return tuple(outs)


def solution(mesh):
    placed = (
        P("dp", "tensor", None),
        P("dp", "tensor", None),
        P(),
        P("dp"),
        P("dp", "tensor"),
        P(None, "tensor"),
        P("dp", "tensor", None),
        P("dp", "tensor", None),
        P("dp", "tensor", None),
    )
    return jax.shard_map(
        work,
        mesh=mesh,
        in_specs=placed,
        out_specs=(P("dp", "tensor", None), P("dp", "tensor", None), P("dp", "tensor", None)),
        check_vma=False,
    )
```

```python
import functools

import jax
import jax.numpy as jnp
from jax import lax
from jax.experimental import pallas as pl
from jax.experimental.pallas import tpu as pltpu
from jax.sharding import PartitionSpec as P


HD = 128
GW = 64


def in_hbm(array):
    return pltpu.with_memory_space_constraint(array, pltpu.HBM)


def visual_kernel(
    here_ref, pos_hbm, gain_hbm, hidden_hbm, cot_hbm, out_ref, pos_ref, gain_ref, held, small, sems
):
    rows = hidden_hbm.shape[1]
    picked = out_ref.shape[0]
    pieces = sems.shape[1]
    piece = rows // pieces
    pos_copy = pltpu.make_async_copy(pos_hbm, pos_ref, small.at[0])
    copies = [pltpu.make_async_copy(gain_hbm, gain_ref, small.at[1])]
    pos_copy.start()
    for i, source in enumerate((hidden_hbm, cot_hbm)):
        for j in range(pieces):
            at = pl.ds(j * piece, piece)
            copies.append(
                pltpu.make_async_copy(source.at[0, at], held.at[i, at], sems.at[i, j])
            )
    for copy in copies:
        copy.start()
    pos_copy.wait()
    row = lax.broadcasted_iota(jnp.int32, (rows, picked), 0) + here_ref[0] * rows
    pick = jnp.where(row == pos_ref[...], 1.0, 0.0).astype(jnp.bfloat16)
    first_both = (((0,), (0,)), ((), ()))
    for copy in copies:
        copy.wait()
    hidden = lax.dot_general(pick, held[0], first_both, preferred_element_type=jnp.float32)
    cot = lax.dot_general(pick, held[1], first_both, preferred_element_type=jnp.float32)
    lanes = gain_ref.shape[1]
    scaled_cot = jnp.concatenate(
        [
            cot[:, j * lanes : (j + 1) * lanes] * gain_ref[pl.ds(j, 1)]
            for j in range(gain_ref.shape[0])
        ],
        axis=1,
    )
    inv_rms = lax.rsqrt(jnp.mean(hidden * hidden, axis=-1, keepdims=True) + 1e-06)
    mixed = jnp.mean(hidden * scaled_cot, axis=-1, keepdims=True)
    out_ref[...] = (inv_rms * scaled_cot - hidden * (inv_rms * inv_rms * inv_rms * mixed)).astype(
        jnp.bfloat16
    )


def visual_grads(here, positions, hidden, cotangent, gain):
    picked, depth = positions.shape[1], hidden.shape[2]
    rows = hidden.shape[1]
    pieces = 8 if rows % 64 == 0 else 1
    vmem = pl.BlockSpec(memory_space=pltpu.VMEM)
    hbm = pl.BlockSpec(memory_space=pltpu.HBM)
    return pl.pallas_call(
        visual_kernel,
        in_specs=[pl.BlockSpec(memory_space=pltpu.SMEM)] + [hbm] * 4,
        out_specs=vmem,
        scratch_shapes=[
            pltpu.VMEM(positions.shape, jnp.int32),
            pltpu.VMEM((depth // HD, HD), jnp.float32),
            pltpu.VMEM((2, rows, depth), jnp.bfloat16),
            pltpu.SemaphoreType.DMA((2,)),
            pltpu.SemaphoreType.DMA((2, pieces)),
        ],
        out_shape=jax.ShapeDtypeStruct((picked, depth), jnp.bfloat16),
        cost_estimate=pl.CostEstimate(
            flops=4 * picked * hidden.size, bytes_accessed=4 * hidden.size, transcendentals=0
        ),
        compiler_params=pltpu.CompilerParams(vmem_limit_bytes=(8 << 20) + 12 * hidden.size),
        name="visual",
    )(here, *map(in_hbm, (positions, gain.reshape(-1, HD), hidden, cotangent)))


def pack_kernel(count, first, slots, here_ref, *refs):
    sources, outs, sems = refs[:3], refs[3:-1], refs[-1]
    width = outs[0].shape[2] // len(slots)
    own_width = sources[0].shape[2] // count
    copies = []
    for k, out in enumerate(outs):
        for j, slot in enumerate(slots):
            column = pl.multiple_of((here_ref[0] ^ k ^ slot) * own_width + first, HD)
            for i in range(out.shape[0]):
                copies.append(
                    pltpu.make_async_copy(
                        sources[i].at[0, :, pl.ds(column, width)],
                        out.at[i, :, pl.ds(j * width, width)],
                        sems.at[len(copies)],
                    )
                )
    for copy in copies:
        copy.start()
    for copy in copies:
        copy.wait()


def pack(here, sources, first, width, slots, taken):
    count, rows = len(taken), sources[0].shape[1]
    total = sum(taken) * len(slots)
    return pl.pallas_call(
        functools.partial(pack_kernel, count, first, slots),
        in_specs=[pl.BlockSpec(memory_space=pltpu.SMEM)]
        + [pl.BlockSpec(memory_space=pltpu.HBM)] * 3,
        out_specs=[pl.BlockSpec(memory_space=pltpu.VMEM)] * count,
        out_shape=[
            jax.ShapeDtypeStruct((n, rows, width * len(slots)), jnp.bfloat16) for n in taken
        ],
        scratch_shapes=[pltpu.SemaphoreType.DMA((total,))],
        cost_estimate=pl.CostEstimate(
            flops=0, bytes_accessed=4 * total * rows * width, transcendentals=0
        ),
        compiler_params=pltpu.CompilerParams(
            vmem_limit_bytes=(1 << 20) + 2 * total * rows * width
        ),
    )(here, *map(in_hbm, sources))


def partners(size, k):
    return [(i, i ^ k) for i in range(size)]


def total_over(value, axis):
    size = lax.axis_size(axis)
    step = 1
    while step < size:
        value = value + lax.ppermute(value, axis, partners(size, step))
        step *= 2
    return value


def gathered(block, axis):
    size = lax.axis_size(axis)
    held = {0: block}
    step = size // 2
    while step:
        for k in sorted(held):
            held[k ^ step] = lax.ppermute(held[k], axis, partners(size, step))
        step //= 2
    return [held[k] for k in range(size)]


def spread_rows(rows, seen):
    token = lax.broadcasted_iota(jnp.int32, (rows, seen), 0)
    source = lax.broadcasted_iota(jnp.int32, (rows, seen), 1)
    return jnp.where(
        (token // (2 * GW)) * (GW // 2) + (token % GW) // 2 == source, 1.0, 0.0
    ).astype(jnp.bfloat16)


BOTH_LAST = (((1,), (1,)), ((), ()))


def attend_kernel(count, scale, chunk, first, skip, *refs):
    handed_ref = refs[0]
    blocks = refs[1 : 1 + count]
    outs = refs[1 + count : 1 + 2 * count]
    q_s, k_s, v_s, g_s, dq_s, dk_s, dv_s = refs[1 + 2 * count :]
    rows = blocks[0].shape[1]
    length = rows * count
    seen = handed_ref.shape[0] // count
    for j, block in enumerate(blocks):
        at = pl.ds(j * rows, rows)
        for i, held in enumerate((q_s, k_s, v_s)):
            held[at] = block[i, :, pl.ds(skip * HD, HD)]
    spread = spread_rows(rows, seen)
    for j in range(count):
        g_s[pl.ds(j * rows, rows)] = jnp.dot(
            spread,
            handed_ref[pl.ds(j * seen, seen), pl.ds(first * HD, HD)],
            preferred_element_type=jnp.float32,
        ).astype(jnp.bfloat16)
    dk_s[...] = jnp.zeros_like(dk_s)
    dv_s[...] = jnp.zeros_like(dv_s)
    key_rows = k_s[...]
    value_rows = v_s[...]
    key_columns = key_rows.T

    def step(c, carry):
        at = pl.ds(pl.multiple_of(c * chunk, chunk), chunk)
        q = q_s[at]
        g = g_s[at]
        scores = lax.dot_general(key_rows, q, BOTH_LAST, preferred_element_type=jnp.float32) * scale
        exp_scores = jnp.exp(scores - jnp.max(scores, axis=0, keepdims=True))
        weights = exp_scores * (1.0 / jnp.sum(exp_scores, axis=0, keepdims=True))
        grad_weights = lax.dot_general(value_rows, g, BOTH_LAST, preferred_element_type=jnp.float32)
        row_dot = jnp.sum(weights * grad_weights, axis=0, keepdims=True)
        grad_scores = (weights * (grad_weights - row_dot)).astype(jnp.bfloat16)
        dv_s[...] += jnp.dot(weights.astype(jnp.bfloat16), g, preferred_element_type=jnp.float32)
        dk_s[...] += jnp.dot(grad_scores, q, preferred_element_type=jnp.float32)
        dq = jnp.dot(key_columns, grad_scores, preferred_element_type=jnp.float32)
        dq_s[at] = (dq * scale).T.astype(jnp.bfloat16)
        return carry

    lax.fori_loop(0, length // chunk, step, 0, unroll=length <= 2 * chunk)
    for j, out in enumerate(outs):
        at = pl.ds(j * rows, rows)
        out[0] = dq_s[at]
        out[1] = (dk_s[at] * scale).astype(jnp.bfloat16)
        out[2] = dv_s[at].astype(jnp.bfloat16)


def attend(handed, blocks, first, skip):
    count = len(blocks)
    rows = blocks[0].shape[1]
    length = rows * count
    chunk = min(256, length)
    vmem = pl.BlockSpec(memory_space=pltpu.VMEM)
    return pl.pallas_call(
        functools.partial(attend_kernel, count, HD**-0.5, chunk, first, skip),
        in_specs=[vmem] * (1 + count),
        out_specs=[vmem] * count,
        scratch_shapes=[pltpu.VMEM((length, HD), jnp.bfloat16)] * 5
        + [pltpu.VMEM((length, HD), jnp.float32)] * 2,
        out_shape=[jax.ShapeDtypeStruct((3, rows, HD), jnp.bfloat16)] * count,
        cost_estimate=pl.CostEstimate(
            flops=10 * length * length * HD,
            bytes_accessed=12 * length * HD,
            transcendentals=length * length,
        ),
        compiler_params=pltpu.CompilerParams(
            vmem_limit_bytes=(6 << 20) + 48 * length * chunk
        ),
    )(handed, *blocks)


def load_half(count, head, heads, first, handed_ref, far_handed_ref, blocks, q_s, k_s, v_s, g_s):
    half, rows = count // 2, blocks[0].shape[1]
    seen = handed_ref.shape[0] // count
    columns = pl.ds(head * HD, HD)
    for j, block in enumerate(blocks):
        at = pl.ds(j * rows, rows)
        q_s[at] = block[0, :, columns]
        if j < half:
            k_s[at] = block[1, :, columns]
            v_s[at] = block[2, :, columns]
    spread = spread_rows(rows, seen)
    each = heads // 2
    if head < each:
        ref, swap, taken = handed_ref, 0, pl.ds((first + head) * HD, HD)
    else:
        ref, swap, taken = far_handed_ref, half, pl.ds((head - each) * HD, HD)
    for j in range(count):
        g_s[pl.ds(j * rows, rows)] = jnp.dot(
            spread, ref[pl.ds((j ^ swap) * seen, seen), taken], preferred_element_type=jnp.float32
        ).astype(jnp.bfloat16)


def half_products(scale, key_rows, value_rows, q, g):
    scores = lax.dot_general(key_rows, q, BOTH_LAST, preferred_element_type=jnp.float32) * scale
    grad_weights = lax.dot_general(value_rows, g, BOTH_LAST, preferred_element_type=jnp.float32)
    return scores, grad_weights


def half_stats_kernel(count, scale, chunk, first, *refs):
    handed_ref, far_handed_ref = refs[:2]
    blocks = refs[2 : 2 + count]
    out = refs[2 + count]
    heads = out.shape[0]
    for head in range(heads):
        q_s, k_s, v_s, g_s = (ref.at[head] for ref in refs[3 + count :])
        load_half(
            count, head, heads, first, handed_ref, far_handed_ref, blocks, q_s, k_s, v_s, g_s
        )
        key_rows, value_rows = k_s[...], v_s[...]

        def step(c, carry):
            at = pl.ds(pl.multiple_of(c * chunk, chunk), chunk)
            scores, grad_weights = half_products(scale, key_rows, value_rows, q_s[at], g_s[at])
            row_max = jnp.max(scores, axis=0, keepdims=True)
            exp_scores = jnp.exp(scores - row_max)
            total = jnp.sum(exp_scores, axis=0, keepdims=True)
            out[head, pl.ds(0, 1), at] = row_max + jnp.log(total)
            out[head, pl.ds(1, 1), at] = (
                jnp.sum(exp_scores * grad_weights, axis=0, keepdims=True) / total
            )
            return carry

        length = q_s.shape[0]
        lax.fori_loop(0, length // chunk, step, 0, unroll=length <= 2 * chunk)


def half_grads_kernel(count, scale, chunk, first, *refs):
    handed_ref, far_handed_ref = refs[:2]
    blocks = refs[2 : 2 + count]
    stats_ref, far_stats_ref = refs[2 + count : 4 + count]
    outs = refs[4 + count : 4 + 2 * count]
    rows = blocks[0].shape[1]
    heads = stats_ref.shape[0]
    for head in range(heads):
        q_s, k_s, v_s, g_s, dq_s, dk_s, dv_s = (ref.at[head] for ref in refs[4 + 2 * count :])
        load_half(
            count, head, heads, first, handed_ref, far_handed_ref, blocks, q_s, k_s, v_s, g_s
        )
        length = q_s.shape[0]
        far_head = (head + heads // 2) % heads
        dk_s[...] = jnp.zeros(dk_s.shape, dk_s.dtype)
        dv_s[...] = jnp.zeros(dv_s.shape, dv_s.dtype)
        key_rows, value_rows = k_s[...], v_s[...]
        key_columns = key_rows.T

        def step(c, carry):
            at = pl.ds(pl.multiple_of(c * chunk, chunk), chunk)
            far_first = lax.rem(c * chunk + length // 2, length)
            far_at = pl.ds(pl.multiple_of(far_first, chunk), chunk)
            q, g = q_s[at], g_s[at]
            scores, grad_weights = half_products(scale, key_rows, value_rows, q, g)
            near = stats_ref[head, pl.ds(0, 1), at]
            far = far_stats_ref[far_head, pl.ds(0, 1), far_at]
            top = jnp.maximum(near, far)
            whole = top + jnp.log(jnp.exp(near - top) + jnp.exp(far - top))
            row_dot = (
                jnp.exp(near - whole) * stats_ref[head, pl.ds(1, 1), at]
                + jnp.exp(far - whole) * far_stats_ref[far_head, pl.ds(1, 1), far_at]
            )
            weights = jnp.exp(scores - whole)
            grad_scores = (weights * (grad_weights - row_dot)).astype(jnp.bfloat16)
            dv_s[...] += jnp.dot(
                weights.astype(jnp.bfloat16), g, preferred_element_type=jnp.float32
            )
            dk_s[...] += jnp.dot(grad_scores, q, preferred_element_type=jnp.float32)
            dq = jnp.dot(key_columns, grad_scores, preferred_element_type=jnp.float32)
            dq_s[at] = (dq * scale).T.astype(jnp.bfloat16)
            return carry

        lax.fori_loop(0, length // chunk, step, 0, unroll=length <= 2 * chunk)
        columns = pl.ds(head * HD, HD)
        for j, out in enumerate(outs):
            at = pl.ds(j * rows, rows)
            out[0, :, columns] = dq_s[at]
            if j < count // 2:
                out[1, :, columns] = (dk_s[at] * scale).astype(jnp.bfloat16)
                out[2, :, columns] = dv_s[at].astype(jnp.bfloat16)


def half_call(kernel, handed, far_handed, blocks, stats, first):
    count = len(blocks)
    rows, heads = blocks[0].shape[1], blocks[0].shape[2] // HD
    length, held = rows * count, rows * count // 2
    chunk = min(256, held)
    vmem = pl.BlockSpec(memory_space=pltpu.VMEM)
    scratch = [pltpu.VMEM((heads, n, HD), jnp.bfloat16) for n in (length, held, held, length)]
    if stats:
        out_specs = [vmem] * count
        out_shape = [jax.ShapeDtypeStruct(b.shape, jnp.bfloat16) for b in blocks]
        scratch += [pltpu.VMEM((heads, length, HD), jnp.bfloat16)]
        scratch += [pltpu.VMEM((heads, held, HD), jnp.float32)] * 2
    else:
        out_specs = vmem
        out_shape = jax.ShapeDtypeStruct((heads, 2, length), jnp.float32)
    return pl.pallas_call(
        functools.partial(kernel, count, HD**-0.5, chunk, first),
        in_specs=[vmem] * (2 + count + len(stats)),
        out_specs=out_specs,
        scratch_shapes=scratch,
        out_shape=out_shape,
        cost_estimate=pl.CostEstimate(
            flops=(10 if stats else 4) * heads * length * held * HD,
            bytes_accessed=12 * length * heads * HD,
            transcendentals=heads * length * held,
        ),
        compiler_params=pltpu.CompilerParams(
            vmem_limit_bytes=(4 << 20) + 12 * heads * length * HD + 80 * length * chunk
        ),
    )(handed, far_handed, *blocks, *stats)


def place_kernel(count, first, *refs):
    here = refs[0][0]
    parts = refs[1 : 1 + count]
    outs = refs[-4:-1]
    sems = refs[-1]
    width = parts[0].shape[2]
    own_width = outs[0].shape[2] // count
    copies = []
    for k, part in enumerate(parts):
        column = pl.multiple_of((here ^ k) * own_width + first, HD)
        for i, out in enumerate(outs):
            copies.append(
                pltpu.make_async_copy(
                    part.at[i], out.at[0, :, pl.ds(column, width)], sems.at[3 * k + i]
                )
            )
    for copy in copies:
        copy.start()
    for copy in copies:
        copy.wait()


def place(here, parts, outs, shape, first):
    count = len(parts)
    anywhere = pl.BlockSpec(memory_space=pl.ANY)
    held = len(outs)
    return pl.pallas_call(
        functools.partial(place_kernel, count, first),
        in_specs=[pl.BlockSpec(memory_space=pltpu.SMEM)]
        + [pl.BlockSpec(memory_space=pltpu.VMEM)] * count
        + [anywhere] * held,
        out_specs=[anywhere] * 3,
        out_shape=[jax.ShapeDtypeStruct(shape, jnp.bfloat16)] * 3,
        input_output_aliases={1 + count + i: i for i in range(held)},
        scratch_shapes=[pltpu.SemaphoreType.DMA((3 * count,))],
        cost_estimate=pl.CostEstimate(
            flops=0, bytes_accessed=4 * count * parts[0].size, transcendentals=0
        ),
        compiler_params=pltpu.CompilerParams(
            vmem_limit_bytes=(1 << 20) + 2 * count * parts[0].size
        ),
    )(here, *parts, *outs)


def place_half_kernel(count, first, *refs):
    here = refs[0][0]
    parts = refs[1 : 1 + count]
    outs = refs[4 + count : 7 + count]
    added, sems = refs[7 + count :]
    half, width = count // 2, parts[0].shape[2] // 2
    own_width = outs[0].shape[2] // count
    copies = []

    def put(source, out, shard):
        column = pl.multiple_of((here ^ shard) * own_width + first, HD)
        copy = pltpu.make_async_copy(
            source, out.at[0, :, pl.ds(column, width)], sems.at[len(copies)]
        )
        copy.start()
        copies.append(copy)

    for k in range(half):
        for slot in range(2):
            for i in (1, 2):
                put(parts[k].at[i, :, pl.ds(slot * width, width)], outs[i], k ^ (half * slot))
    for shard in range(count):
        near = parts[shard][0, :, pl.ds(0, width)].astype(jnp.float32)
        far = parts[shard ^ half][0, :, pl.ds(width, width)].astype(jnp.float32)
        added[shard] = (near + far).astype(jnp.bfloat16)
        put(added.at[shard], outs[0], shard)
    for copy in copies:
        copy.wait()


def place_half(here, parts, outs, first):
    count, (rows, width) = len(parts), parts[0].shape[1:]
    anywhere = pl.BlockSpec(memory_space=pl.ANY)
    return pl.pallas_call(
        functools.partial(place_half_kernel, count, first),
        in_specs=[pl.BlockSpec(memory_space=pltpu.SMEM)]
        + [pl.BlockSpec(memory_space=pltpu.VMEM)] * count
        + [anywhere] * 3,
        out_specs=[anywhere] * 3,
        out_shape=[jax.ShapeDtypeStruct(out.shape, out.dtype) for out in outs],
        input_output_aliases={1 + count + i: i for i in range(3)},
        scratch_shapes=[
            pltpu.VMEM((count, rows, width // 2), jnp.bfloat16),
            pltpu.SemaphoreType.DMA((3 * count,)),
        ],
        cost_estimate=pl.CostEstimate(
            flops=0, bytes_accessed=4 * count * parts[0].size, transcendentals=0
        ),
        compiler_params=pltpu.CompilerParams(
            vmem_limit_bytes=(1 << 20) + 4 * count * parts[0].size
        ),
        name="place_half",
    )(here, *parts, *outs)


def work(
    rm_hidden, rm_cotangent, rm_gain, rewards, visual_pos, bridge, img_query, img_key, img_value
):
    count = lax.axis_size("tensor")
    here = lax.axis_index("tensor")
    place_of = here[None].astype(jnp.int32)
    own_width = img_query.shape[2] // count
    heads = own_width // HD
    shared = heads // 2
    whole = heads - shared
    half = count // 2
    own = (img_query, img_key, img_value)

    def exchange(blocks):
        return [blocks[0]] + [
            lax.ppermute(blocks[k], "tensor", partners(count, k)) for k in range(1, count)
        ]

    visual_grad = visual_grads(place_of, visual_pos, rm_hidden, rm_cotangent, rm_gain)
    visual_blocks = gathered(visual_grad, "tensor")
    if shared:
        taken = (3,) * half + (1,) * half
        packed = pack(place_of, own, whole * HD, shared * HD, (0, half), taken)
        half_blocks = exchange(packed)
    packed = pack(place_of, own, 0, whole * HD, (0,), (3,) * count)
    blocks = exchange(packed)

    reward_sum = total_over(jnp.sum(rewards), "dp")
    sample_count = lax.axis_size("dp") * rewards.shape[0]
    reward_weight = rewards[0] * sample_count / reward_sum
    handed = (
        jnp.dot(
            jnp.concatenate(visual_blocks, axis=0), bridge, preferred_element_type=jnp.float32
        )
        * reward_weight
    ).astype(jnp.bfloat16)
    if shared:
        far_handed = lax.ppermute(handed[:, whole * HD :], "tensor", partners(count, half))

    outs = ()
    for g in range(whole):
        parts = exchange(attend(handed, blocks, g, g))
        outs = place(place_of, parts, outs, img_query.shape, g * HD)
    if shared:
        stats = half_call(half_stats_kernel, handed, far_handed, half_blocks, (), whole)
        far_stats = lax.ppermute(stats, "tensor", partners(count, half))
        grads = half_call(
            half_grads_kernel, handed, far_handed, half_blocks, (stats, far_stats), whole
        )
        outs = place_half(place_of, exchange(grads), outs, whole * HD)
    return tuple(outs)


def solution(mesh):
    placed = (
        P("dp", "tensor", None),
        P("dp", "tensor", None),
        P(),
        P("dp"),
        P("dp", "tensor"),
        P(None, "tensor"),
        P("dp", "tensor", None),
        P("dp", "tensor", None),
        P("dp", "tensor", None),
    )
    return jax.shard_map(
        work,
        mesh=mesh,
        in_specs=placed,
        out_specs=(P("dp", "tensor", None), P("dp", "tensor", None), P("dp", "tensor", None)),
        check_vma=False,
    )
```
